128 devices in a mesh: ctxa: 8 (over x, core), ctxb: 16 (over z, y).
Axes of the slice: x: 4, y: 4, z: 4, core: 2. Of those that a mesh axis runs over, the one named last changes fastest.
Arguments:
- tokens: bfloat16 [65536, 2048], P(('ctxa', 'ctxb')), may hold values from -6 to 6
- cotangent: bfloat16 [65536, 2048], P(('ctxa', 'ctxb')), may hold values from -6 to 6
- w_query: bfloat16 [2048, 1024], replicated, may hold values from -0.125 to 0.125
- w_key: bfloat16 [2048, 1024], replicated, may hold values from -0.125 to 0.125
- w_value: bfloat16 [2048, 1024], replicated, may hold values from -0.125 to 0.125
- w_out: bfloat16 [1024, 2048], replicated, may hold values from -0.125 to 0.125
Outputs:
- grad_tokens: bfloat16 [65536, 2048], P(('ctxa', 'ctxb'))
The draws below stay inside these ranges and needn't reach their ends.
All inputs are finite; a program needn't handle non-finite values.
Results may differ from the reference program's by a relative error of at most 0.012.
Values may be sent and summed in bfloat16 or wider, within the bound.
A program may use at most 256 MiB of HBM per device.

```python
import math
import jax
import jax.numpy as jnp
from jax import lax

D = 2048
H = 8
DH = 128
TOK_DEV = 512
SEQ = 65536


def steps_of(rng, shape, pieces, low, largest):
    gain, own = 1.0, jax.random.fold_in(rng, 6)
    for axis_at, shards_of in pieces:
        draws = jnp.exp(jax.random.uniform(jax.random.fold_in(own, axis_at), (shards_of,), jnp.float32, low / len(pieces), largest / len(pieces)))
        gain = gain * jnp.repeat(draws, shape[axis_at] // shards_of).reshape([-1 if axis == axis_at else 1 for axis in range(len(shape))])
    return gain


def gaussian(key, dims, deviation, bound, split=(), held_as=jnp.bfloat16):
    values = deviation * jax.random.normal(key, dims, jnp.float32)
    if split:
        values = values * steps_of(key, dims, split, -0.22, 0.18)
    return jnp.clip(values, -bound, bound).astype(held_as)


def setup_inputs(seed: int = 0) -> dict:
    key_list = jax.random.split(jax.random.key(seed), 7)
    return {
        "tokens": gaussian(key_list[0], (SEQ, D), 1.0, 6.0, ((0, 128),)),
        "cotangent": gaussian(key_list[1], (SEQ, D), 1.0, 6.0, ((0, 128),)),
        "w_query": gaussian(key_list[2], (D, H * DH), D ** -0.5, 0.125),
        "w_key": gaussian(key_list[3], (D, H * DH), D ** -0.5, 0.125),
        "w_value": gaussian(key_list[4], (D, H * DH), D ** -0.5, 0.125),
        "w_out": gaussian(key_list[5], (H * DH, D), D ** -0.5, 0.125),
    }


def reference(tokens, cotangent, w_query, w_key, w_value, w_out):
    factor = 1.0 / math.sqrt(DH * SEQ)
    blocks = SEQ // TOK_DEV
    query = jnp.dot(tokens, w_query, preferred_element_type=jnp.float32).astype(jnp.bfloat16)
    keys = jnp.dot(tokens, w_key, preferred_element_type=jnp.float32).astype(jnp.bfloat16)
    values = jnp.dot(tokens, w_value, preferred_element_type=jnp.float32).astype(jnp.bfloat16)
    grad_out = jnp.dot(cotangent, w_out.T, preferred_element_type=jnp.float32).astype(jnp.bfloat16)
    query4 = query.reshape(blocks, TOK_DEV, H, DH)
    keys4 = keys.reshape(blocks, TOK_DEV, H, DH)
    values4 = values.reshape(blocks, TOK_DEV, H, DH)
    grad4 = grad_out.reshape(blocks, TOK_DEV, H, DH)
    key_state = jnp.einsum('crhi,crhj->chij', keys4.astype(jnp.float32), values4.astype(jnp.float32))
    grad_state = jnp.einsum('crhi,crhj->chij', query4.astype(jnp.float32), grad4.astype(jnp.float32))
    zero_state = jnp.zeros((1, H, DH, DH), jnp.float32)
    prefix = jnp.concatenate([zero_state, jnp.cumsum(key_state, axis=0)[:-1]], axis=0)
    suffix = jnp.concatenate([jnp.cumsum(grad_state[::-1], axis=0)[:-1][::-1], zero_state], axis=0)
    prefix_bf = prefix.astype(jnp.bfloat16)
    suffix_bf = suffix.astype(jnp.bfloat16)
    index = jnp.arange(TOK_DEV)
    causal = (index[:, None] >= index[None, :])[None]

    def rounded(array):
        return lax.optimization_barrier(array.astype(jnp.bfloat16)).astype(jnp.float32)

    def one_block(items):
        q_block, k_block, v_block, o_block, before, after = items
        q_f = q_block.astype(jnp.float32)
        k_f = k_block.astype(jnp.float32)
        v_f = v_block.astype(jnp.float32)
        o_f = o_block.astype(jnp.float32)
        b_f = before.astype(jnp.float32)
        a_f = after.astype(jnp.float32)
        attend = rounded(jnp.where(causal, jnp.einsum('thi,shi->hts', q_f, k_f), 0.0))
        probe = rounded(jnp.where(causal, jnp.einsum('thj,shj->hts', o_f, v_f), 0.0))
        grad_query = jnp.einsum('hts,shi->thi', probe, k_f) + jnp.einsum('thj,hij->thi', o_f, b_f)
        grad_key = jnp.einsum('hts,thi->shi', probe, q_f) + jnp.einsum('shj,hij->shi', v_f, a_f)
        grad_value = jnp.einsum('hts,thj->shj', attend, o_f) + jnp.einsum('shi,hij->shj', k_f, a_f)
        return ((factor * grad_query).astype(jnp.bfloat16).reshape(TOK_DEV, H * DH), (factor * grad_key).astype(jnp.bfloat16).reshape(TOK_DEV, H * DH), (factor * grad_value).astype(jnp.bfloat16).reshape(TOK_DEV, H * DH))
    grad_query, grad_key, grad_value = lax.map(one_block, (query4, keys4, values4, grad4, prefix_bf, suffix_bf))
    grad_query = grad_query.reshape(SEQ, H * DH)
    grad_key = grad_key.reshape(SEQ, H * DH)
    grad_value = grad_value.reshape(SEQ, H * DH)
    total = jnp.dot(grad_query, w_query.T, preferred_element_type=jnp.float32)
    total = total + jnp.dot(grad_key, w_key.T, preferred_element_type=jnp.float32)
    total = total + jnp.dot(grad_value, w_value.T, preferred_element_type=jnp.float32)
    return total.astype(jnp.bfloat16)
```

```python
import functools
import math

import jax
import jax.numpy as jnp
from jax import lax
from jax.experimental import pallas as pl
from jax.experimental.pallas import tpu as pltpu
from jax.sharding import PartitionSpec as P

MESH = pl.DeviceIdType.MESH
F32 = jnp.float32
BF16 = jnp.bfloat16

DH = 128
PAIR = 2 * DH
PAIRS = 4
SUB = 256
NY = 4
NZ = 4
NA = 8
ROWS = DH // NY
CHUNK = 256


def dot(left, right, left_dim=1, right_dim=0):
    return lax.dot_general(
        left, right, (((left_dim,), (right_dim,)), ((), ())), preferred_element_type=F32
    )


def diagonal(first, second):
    zero = jnp.zeros_like(first)
    return jnp.concatenate(
        [jnp.concatenate([first, zero], axis=1), jnp.concatenate([zero, second], axis=1)], axis=0
    )


def kernel(
    factor,
    tok_h, cot_h, wq_h, wk_h, wv_h, wo_h, out_h,
    tok, cot, wall, wo, qkvg, intra, grads, acc, outs,
    local, sbuf, ybuf, zbuf, xbuf, back, pre,
    load_sem, out_sem,
    y_send, y_recv, z_send, z_recv, x_send, x_recv, b_send, b_recv,
):
    a = lax.axis_index("ctxa")
    b = lax.axis_index("ctxb")
    z, y = b // NY, b % NY

    def y_peer(step):
        return (a, z * NY + (y + step) % NY)

    def z_peer(step):
        return (a, ((z + step) % NZ) * NY + y)

    def x_peer(step):
        return ((a + step) % NA, b)

    barrier = pltpu.get_barrier_semaphore()
    peers = [y_peer(s) for s in range(1, NY)]
    peers += [z_peer(s) for s in range(1, NZ)]
    peers += [x_peer(s) for s in range(1, NA)]

    def columns(p, which):
        return pl.ds(pl.multiple_of((p % 2) * PAIR + which * 2 * PAIR, PAIR), PAIR)

    def weight_loads(p):
        cols = pl.ds(pl.multiple_of(p * PAIR, PAIR), PAIR)
        half = p // 2
        return [
            pltpu.make_async_copy(wk_h.at[:, cols], wall.at[half, :, columns(p, 1)], load_sem.at[p, 0]),
            pltpu.make_async_copy(wv_h.at[:, cols], wall.at[half, :, columns(p, 2)], load_sem.at[p, 1]),
            pltpu.make_async_copy(wq_h.at[:, cols], wall.at[half, :, columns(p, 0)], load_sem.at[p, 2]),
            pltpu.make_async_copy(wo_h.at[cols, :], wo.at[cols, :], load_sem.at[p, 3]),
        ]

    load_tok = pltpu.make_async_copy(tok_h, tok, load_sem.at[PAIRS, 0])
    load_cot = pltpu.make_async_copy(cot_h, cot, load_sem.at[PAIRS, 1])
    first = weight_loads(0)
    load_tok.start()
    first[0].start()
    first[1].start()
    first[2].start()
    load_cot.start()
    first[3].start()

    for peer in peers:
        pl.semaphore_signal(barrier, inc=1, device_id=peer, device_id_type=MESH)

    def y_copy(p, step):
        return pltpu.make_async_remote_copy(
            src_ref=sbuf.at[p, :, (y + step) % NY],
            dst_ref=ybuf.at[p, y],
            send_sem=y_send.at[p, step - 1],
            recv_sem=y_recv.at[p, step - 1],
            device_id=y_peer(step),
            device_id_type=MESH,
        )

    def z_copy(p, step):
        return pltpu.make_async_remote_copy(
            src_ref=zbuf.at[p, z],
            dst_ref=zbuf.at[p, z],
            send_sem=z_send.at[p, step - 1],
            recv_sem=z_recv.at[p, step - 1],
            device_id=z_peer(step),
            device_id_type=MESH,
        )

    def x_copy(p, step):
        return pltpu.make_async_remote_copy(
            src_ref=xbuf.at[p, a],
            dst_ref=xbuf.at[p, a],
            send_sem=x_send.at[p, step - 1],
            recv_sem=x_recv.at[p, step - 1],
            device_id=x_peer(step),
            device_id_type=MESH,
        )

    def b_copy(p, step):
        return pltpu.make_async_remote_copy(
            src_ref=back.at[p, (y + step) % NY],
            dst_ref=pre.at[p, :, y],
            send_sem=b_send.at[p, step - 1],
            recv_sem=b_recv.at[p, step - 1],
            device_id=y_peer(step),
            device_id_type=MESH,
        )

    def start_y(p):
        for step in range(1, NY):
            y_copy(p, step).start()

    def finish_y(p):
        ybuf[p, y] = sbuf[p, :, y]
        for step in range(1, NY):
            y_copy(p, step).wait_recv()
        total = ybuf[p, 0].astype(F32)
        for at in range(1, NY):
            total = total + ybuf[p, at].astype(F32)
        zbuf[p, z] = total.astype(BF16)

    def start_z(p):
        for step in range(1, NZ):
            z_copy(p, step).start()

    def finish_z(p):
        for step in range(1, NZ):
            z_copy(p, step).wait_recv()
        total = zbuf[p, 0].astype(F32)
        for at in range(1, NZ):
            total = total + zbuf[p, at].astype(F32)
        xbuf[p, a] = total.astype(BF16)

    def start_x(p):
        for step in range(1, NA):
            x_copy(p, step).start()

    def finish_x(p):
        for step in range(1, NA):
            x_copy(p, step).wait_recv()
        before = jnp.zeros((2, ROWS, DH), F32)
        after = jnp.zeros((2, ROWS, DH), F32)
        for at in range(NA):
            before = before + jnp.where(at < a, xbuf[p, at, 0:2].astype(F32), 0.0)
            after = after + jnp.where(at > a, xbuf[p, at, 2:4].astype(F32), 0.0)
        for at in range(NZ):
            before = before + jnp.where(at < z, zbuf[p, at, 0:2].astype(F32), 0.0)
            after = after + jnp.where(at > z, zbuf[p, at, 2:4].astype(F32), 0.0)
        for at in range(NY):
            back[p, at, 0:2] = before.astype(BF16)
            before = before + ybuf[p, at, 0:2].astype(F32)
        for at in reversed(range(NY)):
            back[p, at, 2:4] = after.astype(BF16)
            after = after + ybuf[p, at, 2:4].astype(F32)
        pre[p, :, y] = back[p, y]

    def start_b(p):
        for step in range(1, NY):
            b_copy(p, step).start()

    def finish_b(p):
        for step in range(1, NY):
            b_copy(p, step).wait_recv()

    load_tok.wait()

    def states(p, kind, left, right):
        for head in range(2):
            cols = slice(head * DH, (head + 1) * DH)
            parts = [
                dot(left[rows, cols], right[rows, cols], 0, 0)
                for rows in (slice(0, SUB), slice(SUB, 2 * SUB))
            ]
            local[p, 2 * kind + head] = parts[kind]
            total = (parts[0] + parts[1]).astype(BF16)
            sbuf[p, 2 * kind + head] = total.reshape(NY, ROWS, DH)

    def project(p, carry):
        half = p // 2

        @pl.when(p < PAIRS - 1)
        def _():
            for load in weight_loads(p + 1):
                load.start()

        loads = weight_loads(p)
        loads[0].wait()
        keys = dot(tok[...], wall[half, :, columns(p, 1)]).astype(BF16)
        qkvg[p, 1] = keys
        loads[1].wait()
        values = dot(tok[...], wall[half, :, columns(p, 2)]).astype(BF16)
        qkvg[p, 2] = values
        states(p, 0, keys, values)

        @pl.when(p >= 1)
        def _():
            finish_y(p - 1)

        @pl.when(p >= 2)
        def _():
            finish_z(p - 2)

        @pl.when(p >= 3)
        def _():
            finish_x(p - 3)

        loads[2].wait()
        query = dot(tok[...], wall[half, :, columns(p, 0)]).astype(BF16)
        qkvg[p, 0] = query

        @pl.when(p == 0)
        def _():
            pl.semaphore_wait(barrier, len(peers))

        @pl.when(p >= 1)
        def _():
            start_z(p - 1)

        @pl.when(p >= 2)
        def _():
            start_x(p - 2)

        @pl.when(p >= 3)
        def _():
            start_b(p - 3)

        loads[3].wait()

        @pl.when(p == 0)
        def _():
            load_cot.wait()

        rows = pl.ds(pl.multiple_of(p * PAIR, PAIR), PAIR)
        grad_out = dot(cot[...], wo[rows, :], 1, 1).astype(BF16)
        qkvg[p, 3] = grad_out
        states(p, 1, query, grad_out)

        start_y(p)
        return carry

    lax.fori_loop(0, PAIRS, project, 0)

    down = lax.broadcasted_iota(jnp.int32, (SUB, SUB), 0)
    across = lax.broadcasted_iota(jnp.int32, (SUB, SUB), 1)
    lower, upper = down >= across, across >= down

    def attention(p, carry):
        def one(n):
            head, block = n % 2, n // 2
            cols = slice(head * DH, (head + 1) * DH)
            rows = slice(block * SUB, (block + 1) * SUB)
            query, keys = qkvg[p, 0, rows, cols], qkvg[p, 1, rows, cols]
            values, grad_out = qkvg[p, 2, rows, cols], qkvg[p, 3, rows, cols]
            probe = jnp.where(lower, dot(grad_out, values, 1, 1), 0.0).astype(BF16)
            probe_t = jnp.where(upper, dot(values, grad_out, 1, 1), 0.0).astype(BF16)
            attend_t = jnp.where(upper, dot(keys, query, 1, 1), 0.0).astype(BF16)
            intra[p, 0, rows, cols] = dot(probe, keys)
            intra[p, 1, rows, cols] = dot(probe_t, query)
            intra[p, 2, rows, cols] = dot(attend_t, grad_out)

        one(0)
        one(1)

        @pl.when(p == 0)
        def _():
            finish_y(PAIRS - 1)

        @pl.when(p < 2)
        def _():
            finish_z(p + 2)

        @pl.when(p < 3)
        def _():
            finish_x(p + 1)

        one(2)

        @pl.when(p == 0)
        def _():
            start_z(PAIRS - 1)

        @pl.when(p < 2)
        def _():
            start_x(p + 2)

        @pl.when(p < 3)
        def _():
            start_b(p + 1)

        one(3)
        return carry

    lax.fori_loop(0, PAIRS, attention, 0)

    def between(p):
        finish_b(p)
        half = p // 2
        for block in range(2):
            rows = slice(block * SUB, (block + 1) * SUB)
            states_of = [pre[p, n].reshape(DH, DH) for n in range(4)]
            if block == 1:
                before = [(states_of[n].astype(F32) + local[p, n]).astype(BF16) for n in (0, 1)]
                after = states_of[2:]
            else:
                before = states_of[:2]
                after = [(states_of[n].astype(F32) + local[p, n]).astype(BF16) for n in (2, 3)]
            before, after = diagonal(*before), diagonal(*after)
            terms = [
                dot(qkvg[p, 3, rows], before, 1, 1),
                dot(qkvg[p, 2, rows], after, 1, 1),
                dot(qkvg[p, 1, rows], after, 1, 0),
            ]
            for which, term in enumerate(terms):
                grads[half, rows, columns(p, which)] = (
                    factor * (intra[p, which, rows] + term)
                ).astype(BF16)

    lax.fori_loop(0, 2, lambda p, c: (between(p), c)[1], 0)

    steps = wo.shape[1] // CHUNK

    def first_half(n, carry):
        rows = pl.ds(pl.multiple_of(n * CHUNK, CHUNK), CHUNK)
        acc[n] = dot(grads[0], wall[0, rows, :], 1, 1)
        return carry

    lax.fori_loop(0, steps, first_half, 0)
    lax.fori_loop(2, 4, lambda p, c: (between(p), c)[1], 0)

    def out_copy(n):
        cols = pl.ds(pl.multiple_of(n * CHUNK, CHUNK), CHUNK)
        return pltpu.make_async_copy(outs.at[n], out_h.at[:, cols], out_sem.at[n])

    def second_half(n, carry):
        rows = pl.ds(pl.multiple_of(n * CHUNK, CHUNK), CHUNK)
        outs[n] = (acc[n] + dot(grads[1], wall[1, rows, :], 1, 1)).astype(BF16)
        out_copy(n).start()
        return carry

    lax.fori_loop(0, steps, second_half, 0)

    def drain(p, carry):
        for step in range(1, NY):
            y_copy(p, step).wait_send()
            b_copy(p, step).wait_send()
        for step in range(1, NZ):
            z_copy(p, step).wait_send()
        for step in range(1, NA):
            x_copy(p, step).wait_send()
        return carry

    lax.fori_loop(0, PAIRS, drain, 0)
    lax.fori_loop(0, steps, lambda n, c: (out_copy(n).wait(), c)[1], 0)


def shards(tokens, cotangent, w_query, w_key, w_value, w_out):
    rows, width = tokens.shape
    blocks = lax.axis_size("ctxa") * lax.axis_size("ctxb")
    factor = 1.0 / math.sqrt(DH * rows * blocks)
    steps = width // CHUNK
    slot = (4, ROWS, DH)
    dma = pltpu.SemaphoreType.DMA
    return pl.pallas_call(
        functools.partial(kernel, factor),
        out_shape=jax.ShapeDtypeStruct((rows, width), BF16),
        in_specs=[pl.BlockSpec(memory_space=pl.ANY)] * 6,
        out_specs=pl.BlockSpec(memory_space=pl.ANY),
        scratch_shapes=[
            pltpu.VMEM((rows, width), BF16),
            pltpu.VMEM((rows, width), BF16),
            pltpu.VMEM((2, width, 6 * PAIR), BF16),
            pltpu.VMEM((PAIRS * PAIR, width), BF16),
            pltpu.VMEM((PAIRS, 4, rows, PAIR), BF16),
            pltpu.VMEM((PAIRS, 3, rows, PAIR), F32),
            pltpu.VMEM((2, rows, 6 * PAIR), BF16),
            pltpu.VMEM((steps, rows, CHUNK), F32),
            pltpu.VMEM((steps, rows, CHUNK), BF16),
            pltpu.VMEM((PAIRS, 4, DH, DH), F32),
            pltpu.VMEM((PAIRS, 4, NY, ROWS, DH), BF16),
            pltpu.VMEM((PAIRS, NY, *slot), BF16),
            pltpu.VMEM((PAIRS, NZ, *slot), BF16),
            pltpu.VMEM((PAIRS, NA, *slot), BF16),
            pltpu.VMEM((PAIRS, NY, *slot), BF16),
            pltpu.VMEM((PAIRS, 4, NY, ROWS, DH), BF16),
            dma((PAIRS + 1, 4)),
            dma((steps,)),
            dma((PAIRS, NY - 1)),
            dma((PAIRS, NY - 1)),
            dma((PAIRS, NZ - 1)),
            dma((PAIRS, NZ - 1)),
            dma((PAIRS, NA - 1)),
            dma((PAIRS, NA - 1)),
            dma((PAIRS, NY - 1)),
            dma((PAIRS, NY - 1)),
        ],
        compiler_params=pltpu.CompilerParams(
            collective_id=0, has_side_effects=True, vmem_limit_bytes=60 * 1024 * 1024
        ),
    )(tokens, cotangent, w_query, w_key, w_value, w_out)


def solution(mesh):
    placed = (P(("ctxa", "ctxb"), None), P(("ctxa", "ctxb"), None), P(), P(), P(), P())
    return jax.shard_map(
        shards, mesh=mesh, in_specs=placed, out_specs=P(("ctxa", "ctxb"), None), check_vma=False
    )
```

```python
import functools
import math

import jax
import jax.numpy as jnp
from jax import lax
from jax.experimental import pallas as pl
from jax.experimental.pallas import tpu as pltpu
from jax.sharding import PartitionSpec as P

MESH = pl.DeviceIdType.MESH
F32 = jnp.float32
BF16 = jnp.bfloat16

DH = 128
PAIR = 2 * DH
PAIRS = 4
SUB = 256
NY = 4
NZ = 4
NA = 8
ROWS = DH // NY
CHUNK = 512
EARLY = 3 * 3 * PAIR


def dot(left, right, left_dim=1, right_dim=0):
    return lax.dot_general(
        left, right, (((left_dim,), (right_dim,)), ((), ())), preferred_element_type=F32
    )


def diagonal(first, second):
    zero = jnp.zeros_like(first)
    return jnp.concatenate(
        [jnp.concatenate([first, zero], axis=1), jnp.concatenate([zero, second], axis=1)], axis=0
    )


def kernel(
    factor,
    tok_h, cot_h, wq_h, wk_h, wv_h, wo_h, out,
    tok, cot, wall, wo, qkvg, intra, grads, acc,
    local, sbuf, ybuf, zbuf, xown, xbuf, back, pre,
    load_sem,
    y_send, y_recv, z_send, z_recv, x_send, x_recv, b_send, b_recv,
):
    a = lax.axis_index("ctxa")
    b = lax.axis_index("ctxb")
    z, y = b // NY, b % NY

    def y_peer(step):
        return (a, z * NY + (y + step) % NY)

    def z_peer(step):
        return (a, ((z + step) % NZ) * NY + y)

    def x_peer(step):
        return ((a + step) % NA, b)

    barrier = pltpu.get_barrier_semaphore()
    peers = [y_peer(s) for s in range(1, NY)]
    peers += [z_peer(s) for s in range(1, NZ)]
    peers += [x_peer(s) for s in range(1, NA)]

    def columns(p, which, count=1):
        return slice((3 * p + which) * PAIR, (3 * p + which + count) * PAIR)

    def weight(p, which):
        cols = slice(p * PAIR, (p + 1) * PAIR)
        if which == 3:
            return pltpu.make_async_copy(wo_h.at[cols, :], wo.at[cols, :], load_sem.at[4 * p + 3])
        source = (wq_h, wk_h, wv_h)[which]
        return pltpu.make_async_copy(
            source.at[:, cols], wall.at[:, columns(p, which)], load_sem.at[4 * p + which]
        )

    load_tok = pltpu.make_async_copy(tok_h, tok, load_sem.at[4 * PAIRS])
    load_cot = pltpu.make_async_copy(cot_h, cot, load_sem.at[4 * PAIRS + 1])
    loads = [
        [load_tok, weight(0, 1), weight(0, 2)],
        [weight(1, 1), weight(1, 2)],
        [load_cot, weight(0, 0), weight(0, 3)],
        [weight(1, 0), weight(1, 3)],
        [weight(2, 1), weight(2, 2)],
        [weight(3, 1), weight(3, 2)],
        [weight(2, 0), weight(2, 3)],
        [weight(3, 0), weight(3, 3)],
    ]

    def fetch(*groups):
        for group in groups:
            for load in loads[group]:
                load.start()

    def arrive(group):
        for load in loads[group]:
            load.wait()

    def remote(source, target, sent, received, device):
        return pltpu.make_async_remote_copy(
            src_ref=source, dst_ref=target, send_sem=sent, recv_sem=received,
            device_id=device, device_id_type=MESH,
        )

    def y_copy(p, step):
        return remote(
            sbuf.at[p, :, (y + step) % NY], ybuf.at[p, y],
            y_send.at[p, step - 1], y_recv.at[p, step - 1], y_peer(step),
        )

    def z_copy(p, step):
        return remote(
            zbuf.at[p, z], zbuf.at[p, z],
            z_send.at[p, step - 1], z_recv.at[p, step - 1], z_peer(step),
        )

    def x_copy(p, step):
        return remote(
            xown.at[p, (a + step) // NA], xbuf.at[p, a],
            x_send.at[p, step - 1], x_recv.at[p, step - 1], x_peer(step),
        )

    def b_copy(p, step):
        return remote(
            back.at[p, (y + step) % NY], pre.at[p, :, y],
            b_send.at[p, step - 1], b_recv.at[p, step - 1], y_peer(step),
        )

    def start(copy, count, p):
        for step in range(1, count):
            copy(p, step).start()

    def receive(copy, count, p):
        for step in range(1, count):
            copy(p, step).wait_recv()

    def finish_y(p):
        receive(y_copy, NY, p)
        ybuf[p, y] = sbuf[p, :, y]
        total = ybuf[p, 0].astype(F32)
        for at in range(1, NY):
            total = total + ybuf[p, at].astype(F32)
        zbuf[p, z] = total.astype(BF16)

    def finish_z(p):
        receive(z_copy, NZ, p)
        total = zbuf[p, 0].astype(F32)
        for at in range(1, NZ):
            total = total + zbuf[p, at].astype(F32)
        total = total.astype(BF16)
        xown[p, 0] = total[0:2]
        xown[p, 1] = total[2:4]

    def finish_x(p):
        receive(x_copy, NA, p)
        before = jnp.zeros((2, ROWS, DH), F32)
        after = jnp.zeros((2, ROWS, DH), F32)
        for at in range(NA):
            part = xbuf[p, at].astype(F32)
            before = before + jnp.where(at < a, part, 0.0)
            after = after + jnp.where(at > a, part, 0.0)
        for at in range(NZ):
            before = before + jnp.where(at < z, zbuf[p, at, 0:2].astype(F32), 0.0)
            after = after + jnp.where(at > z, zbuf[p, at, 2:4].astype(F32), 0.0)
        for at in range(NY):
            back[p, at, 0:2] = before.astype(BF16)
            before = before + ybuf[p, at, 0:2].astype(F32)
        for at in reversed(range(NY)):
            back[p, at, 2:4] = after.astype(BF16)
            after = after + ybuf[p, at, 2:4].astype(F32)
        pre[p, :, y] = back[p, y]

    def start_y(p):
        start(y_copy, NY, p)

    def start_z(p):
        start(z_copy, NZ, p)

    def start_x(p):
        start(x_copy, NA, p)

    def start_b(p):
        start(b_copy, NY, p)

    def states(p, kind, left, right):
        for head in range(2):
            cols = slice(head * DH, (head + 1) * DH)
            parts = [
                dot(left[rows, cols], right[rows, cols], 0, 0)
                for rows in (slice(0, SUB), slice(SUB, 2 * SUB))
            ]
            local[p, 2 * kind + head] = parts[kind]
            total = (parts[0] + parts[1]).astype(BF16)
            sbuf[p, 2 * kind + head] = total.reshape(NY, ROWS, DH)

    def keys_values(p):
        both = dot(tok[...], wall[:, columns(p, 1, 2)]).astype(BF16)
        keys, values = both[:, :PAIR], both[:, PAIR:]
        qkvg[p, 1] = keys
        qkvg[p, 2] = values
        states(p, 0, keys, values)

    def query_grad(p):
        query = dot(tok[...], wall[:, columns(p, 0)]).astype(BF16)
        grad_out = dot(cot[...], wo[p * PAIR : (p + 1) * PAIR], 1, 1).astype(BF16)
        qkvg[p, 0] = query
        qkvg[p, 3] = grad_out
        states(p, 1, query, grad_out)

    down = lax.broadcasted_iota(jnp.int32, (SUB, SUB), 0)
    across = lax.broadcasted_iota(jnp.int32, (SUB, SUB), 1)
    lower, upper = down >= across, across >= down

    def attention(p):
        for block in range(2):
            for head in range(2):
                cols = slice(head * DH, (head + 1) * DH)
                rows = slice(block * SUB, (block + 1) * SUB)
                query, keys = qkvg[p, 0, rows, cols], qkvg[p, 1, rows, cols]
                values, grad_out = qkvg[p, 2, rows, cols], qkvg[p, 3, rows, cols]
                probe = jnp.where(lower, dot(grad_out, values, 1, 1), 0.0).astype(BF16)
                probe_t = jnp.where(upper, dot(values, grad_out, 1, 1), 0.0).astype(BF16)
                attend_t = jnp.where(upper, dot(keys, query, 1, 1), 0.0).astype(BF16)
                intra[p, 0, rows, cols] = dot(probe, keys)
                intra[p, 1, rows, cols] = dot(probe_t, query)
                intra[p, 2, rows, cols] = dot(attend_t, grad_out)

    def between(p):
        states_of = [pre[p, n].reshape(DH, DH) for n in range(4)]
        for block in range(2):
            rows = slice(block * SUB, (block + 1) * SUB)
            own = (0, 1) if block == 1 else (2, 3)
            moved = [
                (states_of[n].astype(F32) + local[p, n]).astype(BF16) if n in own else states_of[n]
                for n in range(4)
            ]
            before, after = diagonal(*moved[:2]), diagonal(*moved[2:])
            terms = [
                dot(qkvg[p, 3, rows], before, 1, 1),
                dot(qkvg[p, 2, rows], after, 1, 1),
                dot(qkvg[p, 1, rows], after, 1, 0),
            ]
            for which, term in enumerate(terms):
                grads[rows, columns(p, which)] = (
                    factor * (intra[p, which, rows] + term)
                ).astype(BF16)

    def early(n):
        acc[n] = dot(grads[:, :EARLY], wall[n * CHUNK : (n + 1) * CHUNK, :EARLY], 1, 1)

    def late(n):
        part = dot(grads[:, EARLY:], wall[n * CHUNK : (n + 1) * CHUNK, EARLY:], 1, 1)
        out[:, n * CHUNK : (n + 1) * CHUNK] = (acc[n] + part).astype(BF16)

    fetch(0)
    for peer in peers:
        pl.semaphore_signal(barrier, inc=1, device_id=peer, device_id_type=MESH)
    arrive(0)
    fetch(1, 2)
    keys_values(0)

    arrive(1)
    fetch(3)
    keys_values(1)

    arrive(2)
    fetch(4)
    query_grad(0)

    arrive(3)
    fetch(5, 6, 7)
    pl.semaphore_wait(barrier, len(peers))
    start_y(0)
    query_grad(1)

    arrive(4)
    start_y(1)
    keys_values(2)

    arrive(5)
    finish_y(0)
    start_z(0)
    keys_values(3)

    arrive(6)
    finish_y(1)
    start_z(1)
    query_grad(2)

    arrive(7)
    finish_z(0)
    start_x(0)
    start_y(2)
    query_grad(3)

    finish_z(1)
    start_x(1)
    start_y(3)
    attention(0)

    finish_y(2)
    finish_x(0)
    start_z(2)
    start_b(0)
    attention(1)

    finish_y(3)
    finish_x(1)
    start_z(3)
    start_b(1)
    attention(2)

    finish_z(2)
    start_x(2)
    attention(3)

    finish_z(3)
    receive(b_copy, NY, 0)
    start_x(3)
    between(0)
    receive(b_copy, NY, 1)
    between(1)

    finish_x(2)
    start_b(2)
    receive(b_copy, NY, 2)
    between(2)
    finish_x(3)
    start_b(3)

    for n in range(4):
        early(n)
    receive(b_copy, NY, 3)
    between(3)
    for n in range(4):
        late(n)

    for p in range(PAIRS):
        for copy, count in ((y_copy, NY), (z_copy, NZ), (x_copy, NA), (b_copy, NY)):
            for step in range(1, count):
                copy(p, step).wait_send()


def shards(tokens, cotangent, w_query, w_key, w_value, w_out):
    rows, width = tokens.shape
    blocks = lax.axis_size("ctxa") * lax.axis_size("ctxb")
    factor = 1.0 / math.sqrt(DH * rows * blocks)
    slot = (4, ROWS, DH)
    half = (2, ROWS, DH)
    dma = pltpu.SemaphoreType.DMA
    return pl.pallas_call(
        functools.partial(kernel, factor),
        out_shape=pltpu.VMEM((rows, width), BF16),
        in_specs=[pl.BlockSpec(memory_space=pl.ANY)] * 6,
        out_specs=pl.BlockSpec(memory_space=pltpu.VMEM),
        scratch_shapes=[
            pltpu.VMEM((rows, width), BF16),
            pltpu.VMEM((rows, width), BF16),
            pltpu.VMEM((width, 3 * PAIRS * PAIR), BF16),
            pltpu.VMEM((PAIRS * PAIR, width), BF16),
            pltpu.VMEM((PAIRS, 4, rows, PAIR), BF16),
            pltpu.VMEM((PAIRS, 3, rows, PAIR), F32),
            pltpu.VMEM((rows, 3 * PAIRS * PAIR), BF16),
            pltpu.VMEM((width // CHUNK, rows, CHUNK), F32),
            pltpu.VMEM((PAIRS, 4, DH, DH), F32),
            pltpu.VMEM((PAIRS, 4, NY, ROWS, DH), BF16),
            pltpu.VMEM((PAIRS, NY, *slot), BF16),
            pltpu.VMEM((PAIRS, NZ, *slot), BF16),
            pltpu.VMEM((PAIRS, 2, *half), BF16),
            pltpu.VMEM((PAIRS, NA, *half), BF16),
            pltpu.VMEM((PAIRS, NY, *slot), BF16),
            pltpu.VMEM((PAIRS, 4, NY, ROWS, DH), BF16),
            dma((4 * PAIRS + 2,)),
            dma((PAIRS, NY - 1)),
            dma((PAIRS, NY - 1)),
            dma((PAIRS, NZ - 1)),
            dma((PAIRS, NZ - 1)),
            dma((PAIRS, NA - 1)),
            dma((PAIRS, NA - 1)),
            dma((PAIRS, NY - 1)),
            dma((PAIRS, NY - 1)),
        ],
        compiler_params=pltpu.CompilerParams(
            collective_id=0, has_side_effects=True, vmem_limit_bytes=56 * 1024 * 1024
        ),
    )(tokens, cotangent, w_query, w_key, w_value, w_out)


def solution(mesh):
    placed = (P(("ctxa", "ctxb"), None), P(("ctxa", "ctxb"), None), P(), P(), P(), P())
    return jax.shard_map(
        shards, mesh=mesh, in_specs=placed, out_specs=P(("ctxa", "ctxb"), None), check_vma=False
    )
```

```python
import functools
import math

import jax
import jax.numpy as jnp
from jax import lax
from jax.experimental import pallas as pl
from jax.experimental.pallas import tpu as pltpu
from jax.sharding import PartitionSpec as P

MESH = pl.DeviceIdType.MESH
F32 = jnp.float32
BF16 = jnp.bfloat16

DH = 128
PAIR = 2 * DH
PAIRS = 4
SUB = 256
NY = 4
NZ = 4
NA = 8
ROWS = DH // NY
CHUNK = 512
KEYS, GRADS = 0, PAIRS


K, G = KEYS, GRADS
ORDER = (
    ("got", 1), ("get", 3), ("ys", K), ("kv", 1),
    ("got", 2), ("get", 4), ("ys", K + 1), ("kv", 2),
    ("got", 3), ("get", 5), ("ys", K + 2), ("kv", 3),
    ("got", 4), ("get", 6), ("ys", K + 3), ("yf", K), ("zs", K), ("qg", 0),
    ("got", 5), ("get", 7), ("ys", G), ("yf", K + 1), ("zs", K + 1), ("qg", 1),
    ("got", 6), ("ys", G + 1), ("yf", K + 2), ("zs", K + 2), ("qg", 2),
    ("got", 7), ("ys", G + 2), ("yf", K + 3), ("zf", K), ("zs", K + 3), ("xs", K), ("qg", 3),
    ("ys", G + 3), ("yf", G), ("zf", K + 1), ("zs", G), ("xs", K + 1), ("a", 0),
    ("yf", G + 1), ("zf", K + 2), ("zs", G + 1), ("xs", K + 2), ("a", 1),
    ("yf", G + 2), ("zf", K + 3), ("xf", K), ("zs", G + 2), ("xs", K + 3), ("bs", K), ("a", 2),
    ("yf", G + 3), ("zf", G), ("xf", K + 1), ("zs", G + 3), ("xs", G), ("bs", K + 1), ("a", 3),
    ("zf", G + 1), ("xf", K + 2), ("xs", G + 1), ("bs", K + 2), ("bf", K), ("bq", 0), ("pq", 0),
    ("zf", G + 2), ("xf", K + 3), ("xs", G + 2), ("bs", K + 3), ("bf", K + 1), ("bq", 1), ("pq", 1),
    ("zf", G + 3), ("xf", G), ("xs", G + 3), ("bs", G), ("bf", K + 2), ("bq", 2), ("pq", 2),
    ("xf", G + 1), ("bs", G + 1), ("bf", K + 3), ("bq", 3), ("pq", 3),
    ("xf", G + 2), ("bs", G + 2), ("bf", G), ("br", 0), ("pr", 0),
    ("xf", G + 3), ("bs", G + 3), ("bf", G + 1), ("br", 1), ("pr", 1),
    ("bf", G + 2), ("br", 2), ("pr", 2),
    ("bf", G + 3), ("br", 3), ("pr", 3),
)


def dot(left, right, left_dim=1, right_dim=0):
    return lax.dot_general(
        left, right, (((left_dim,), (right_dim,)), ((), ())), preferred_element_type=F32
    )


def diagonal(first, second):
    zero = jnp.zeros_like(first)
    return jnp.concatenate(
        [jnp.concatenate([first, zero], axis=1), jnp.concatenate([zero, second], axis=1)], axis=0
    )


def kernel(
    factor,
    tok_h, cot_h, wq_h, wk_h, wv_h, wo_h, out,
    tok, cot, wall, wo, qkvg, intra, grads, acc,
    local, sbuf, ybuf, zbuf, xown, xbuf, back, pre,
    load_sem,
    y_send, y_recv, z_send, z_recv, x_send, x_recv, b_send, b_recv,
):
    a = lax.axis_index("ctxa")
    b = lax.axis_index("ctxb")
    z, y = b // NY, b % NY

    def y_peer(step):
        return (a, z * NY + (y + step) % NY)

    def z_peer(step):
        return (a, ((z + step) % NZ) * NY + y)

    def x_peer(step):
        return ((a + step) % NA, b)

    barrier = pltpu.get_barrier_semaphore()
    peers = [y_peer(s) for s in range(1, NY)]
    peers += [z_peer(s) for s in range(1, NZ)]
    peers += [x_peer(s) for s in range(1, NA)]

    def columns(p, which, count=1):
        first = p if which == 0 else PAIRS + 2 * p + which - 1
        return slice(first * PAIR, (first + count) * PAIR)

    def weight(p, which):
        cols = slice(p * PAIR, (p + 1) * PAIR)
        if which == 3:
            return pltpu.make_async_copy(wo_h.at[cols, :], wo.at[cols, :], load_sem.at[4 * p + 3])
        source = (wq_h, wk_h, wv_h)[which]
        return pltpu.make_async_copy(
            source.at[:, cols], wall.at[:, columns(p, which)], load_sem.at[4 * p + which]
        )

    load_tok = pltpu.make_async_copy(tok_h, tok, load_sem.at[4 * PAIRS])
    load_cot = pltpu.make_async_copy(cot_h, cot, load_sem.at[4 * PAIRS + 1])
    loads = [[load_tok, weight(0, 1), weight(0, 2)]]
    loads += [[weight(p, 1), weight(p, 2)] for p in range(1, PAIRS)]
    loads += [[load_cot, weight(0, 0), weight(0, 3)]]
    loads += [[weight(p, 0), weight(p, 3)] for p in range(1, PAIRS)]

    def fetch(group):
        for load in loads[group]:
            load.start()

    def arrive(group):
        for load in loads[group]:
            load.wait()

    def remote(source, target, sent, received, device):
        return pltpu.make_async_remote_copy(
            src_ref=source, dst_ref=target, send_sem=sent, recv_sem=received,
            device_id=device, device_id_type=MESH,
        )

    def y_copy(m, step):
        return remote(
            sbuf.at[m, :, (y + step) % NY], ybuf.at[m, y],
            y_send.at[m, step - 1], y_recv.at[m, step - 1], y_peer(step),
        )

    def z_copy(m, step):
        return remote(
            zbuf.at[m, z], zbuf.at[m, z],
            z_send.at[m, step - 1], z_recv.at[m, step - 1], z_peer(step),
        )

    def x_copy(m, step):
        return remote(
            xown.at[m], xbuf.at[m, a],
            x_send.at[m, step - 1], x_recv.at[m, step - 1], x_peer(step if m < GRADS else NA - step),
        )

    def b_copy(m, step):
        return remote(
            back.at[m, (y + step) % NY], pre.at[m, :, y],
            b_send.at[m, step - 1], b_recv.at[m, step - 1], y_peer(step),
        )

    def start(copy, count, m):
        for step in range(1, count):
            copy(m, step).start()

    def receive(copy, count, m):
        for step in range(1, count):
            copy(m, step).wait_recv()

    def x_each(m, sending, act):
        upward = (m < GRADS) == sending
        for step in range(1, NA):
            pl.when(a + step < NA if upward else a >= step)(functools.partial(act, m, step))

    def start_y(m):
        start(y_copy, NY, m)

    def start_z(m):
        start(z_copy, NZ, m)

    def start_x(m):
        x_each(m, True, lambda m, step: x_copy(m, step).start())

    def start_b(m):
        start(b_copy, NY, m)

    def finish_y(m):
        receive(y_copy, NY, m)
        ybuf[m, y] = sbuf[m, :, y]
        total = ybuf[m, 0].astype(F32)
        for at in range(1, NY):
            total = total + ybuf[m, at].astype(F32)
        zbuf[m, z] = total.astype(BF16)

    def finish_z(m):
        receive(z_copy, NZ, m)
        total = zbuf[m, 0].astype(F32)
        for at in range(1, NZ):
            total = total + zbuf[m, at].astype(F32)
        xown[m] = total.astype(BF16)

    def finish_x(m):
        x_each(m, False, lambda m, step: x_copy(m, step).wait_recv())
        keys = m < GRADS
        total = jnp.zeros((2, ROWS, DH), F32)
        for at in range(NA):
            total = total + jnp.where(at < a if keys else at > a, xbuf[m, at].astype(F32), 0.0)
        for at in range(NZ):
            total = total + jnp.where(at < z if keys else at > z, zbuf[m, at].astype(F32), 0.0)
        for at in range(NY) if keys else reversed(range(NY)):
            back[m, at] = total.astype(BF16)
            total = total + ybuf[m, at].astype(F32)
        pre[m, :, y] = back[m, y]

    def finish_b(m):
        receive(b_copy, NY, m)

    def states(p, kind, left, right):
        for head in range(2):
            cols = slice(head * DH, (head + 1) * DH)
            parts = [
                dot(left[rows, cols], right[rows, cols], 0, 0)
                for rows in (slice(0, SUB), slice(SUB, 2 * SUB))
            ]
            m = kind * PAIRS + p
            local[m, head] = parts[kind]
            sbuf[m, head] = (parts[0] + parts[1]).astype(BF16).reshape(NY, ROWS, DH)

    def keys_values(p):
        both = dot(tok[...], wall[:, columns(p, 1, 2)]).astype(BF16)
        keys, values = both[:, :PAIR], both[:, PAIR:]
        qkvg[p, 1] = keys
        qkvg[p, 2] = values
        states(p, 0, keys, values)

    def query_grad(p):
        query = dot(tok[...], wall[:, columns(p, 0)]).astype(BF16)
        grad_out = dot(cot[...], wo[p * PAIR : (p + 1) * PAIR], 1, 1).astype(BF16)
        qkvg[p, 0] = query
        qkvg[p, 3] = grad_out
        states(p, 1, query, grad_out)

    down = lax.broadcasted_iota(jnp.int32, (SUB, SUB), 0)
    across = lax.broadcasted_iota(jnp.int32, (SUB, SUB), 1)
    lower, upper = down >= across, across >= down

    def attention(p):
        for block in range(2):
            for head in range(2):
                cols = slice(head * DH, (head + 1) * DH)
                rows = slice(block * SUB, (block + 1) * SUB)
                query, keys = qkvg[p, 0, rows, cols], qkvg[p, 1, rows, cols]
                values, grad_out = qkvg[p, 2, rows, cols], qkvg[p, 3, rows, cols]
                probe = jnp.where(lower, dot(grad_out, values, 1, 1), 0.0).astype(BF16)
                probe_t = jnp.where(upper, dot(values, grad_out, 1, 1), 0.0).astype(BF16)
                attend_t = jnp.where(upper, dot(keys, query, 1, 1), 0.0).astype(BF16)
                intra[p, 0, rows, cols] = dot(probe, keys)
                intra[p, 1, rows, cols] = dot(probe_t, query)
                intra[p, 2, rows, cols] = dot(attend_t, grad_out)

    def moved(m, block):
        whole = [pre[m, head].reshape(DH, DH) for head in range(2)]
        if block == (1 if m < GRADS else 0):
            whole = [(whole[head].astype(F32) + local[m, head]).astype(BF16) for head in range(2)]
        return diagonal(*whole)

    def finish(p, which, rows, term):
        grads[rows, columns(p, which)] = (factor * (intra[p, which, rows] + term)).astype(BF16)

    def between_query(p):
        for block in range(2):
            rows = slice(block * SUB, (block + 1) * SUB)
            finish(p, 0, rows, dot(qkvg[p, 3, rows], moved(KEYS + p, block), 1, 1))

    def between_rest(p):
        for block in range(2):
            rows = slice(block * SUB, (block + 1) * SUB)
            after = moved(GRADS + p, block)
            finish(p, 1, rows, dot(qkvg[p, 2, rows], after, 1, 1))
            finish(p, 2, rows, dot(qkvg[p, 1, rows], after, 1, 0))

    def product(cols, first=False, last=False):
        for n in range(acc.shape[0]):
            rows = slice(n * CHUNK, (n + 1) * CHUNK)
            part = dot(grads[:, cols], wall[rows, cols], 1, 1)
            part = part if first else acc[n] + part
            if last:
                out[:, rows] = part.astype(BF16)
            else:
                acc[n] = part

    blocks = {
        "kv": keys_values, "qg": query_grad, "a": attention, "bq": between_query, "br": between_rest,
        "yf": finish_y, "zf": finish_z, "xf": finish_x, "bf": finish_b,
        "ys": start_y, "zs": start_z, "xs": start_x, "bs": start_b,
        "get": fetch, "got": arrive,
        "pq": lambda p: product(columns(p, 0), first=p == 0),
        "pr": lambda p: product(columns(p, 1, 2), last=p == PAIRS - 1),
    }

    fetch(0)
    for peer in peers:
        pl.semaphore_signal(barrier, inc=1, device_id=peer, device_id_type=MESH)
    arrive(0)
    fetch(1)
    fetch(2)
    keys_values(0)
    pl.semaphore_wait(barrier, len(peers))
    for name, at in ORDER:
        blocks[name](at)

    for m in range(2 * PAIRS):
        for copy, count in ((y_copy, NY), (z_copy, NZ), (b_copy, NY)):
            for step in range(1, count):
                copy(m, step).wait_send()
        x_each(m, True, lambda m, step: x_copy(m, step).wait_send())


def shards(tokens, cotangent, w_query, w_key, w_value, w_out):
    rows, width = tokens.shape
    blocks = lax.axis_size("ctxa") * lax.axis_size("ctxb")
    factor = 1.0 / math.sqrt(DH * rows * blocks)
    slot = (2, ROWS, DH)
    messages = 2 * PAIRS
    dma = pltpu.SemaphoreType.DMA
    return pl.pallas_call(
        functools.partial(kernel, factor),
        out_shape=pltpu.VMEM((rows, width), BF16),
        in_specs=[pl.BlockSpec(memory_space=pl.ANY)] * 6,
        out_specs=pl.BlockSpec(memory_space=pltpu.VMEM),
        scratch_shapes=[
            pltpu.VMEM((rows, width), BF16),
            pltpu.VMEM((rows, width), BF16),
            pltpu.VMEM((width, 3 * PAIRS * PAIR), BF16),
            pltpu.VMEM((PAIRS * PAIR, width), BF16),
            pltpu.VMEM((PAIRS, 4, rows, PAIR), BF16),
            pltpu.VMEM((PAIRS, 3, rows, PAIR), F32),
            pltpu.VMEM((rows, 3 * PAIRS * PAIR), BF16),
            pltpu.VMEM((width // CHUNK, rows, CHUNK), F32),
            pltpu.VMEM((messages, 2, DH, DH), F32),
            pltpu.VMEM((messages, 2, NY, ROWS, DH), BF16),
            pltpu.VMEM((messages, NY, *slot), BF16),
            pltpu.VMEM((messages, NZ, *slot), BF16),
            pltpu.VMEM((messages, *slot), BF16),
            pltpu.VMEM((messages, NA, *slot), BF16),
            pltpu.VMEM((messages, NY, *slot), BF16),
            pltpu.VMEM((messages, 2, NY, ROWS, DH), BF16),
            dma((4 * PAIRS + 2,)),
            dma((messages, NY - 1)),
            dma((messages, NY - 1)),
            dma((messages, NZ - 1)),
            dma((messages, NZ - 1)),
            dma((messages, NA - 1)),
            dma((messages, NA - 1)),
            dma((messages, NY - 1)),
            dma((messages, NY - 1)),
        ],
        compiler_params=pltpu.CompilerParams(
            collective_id=0, has_side_effects=True, vmem_limit_bytes=56 * 1024 * 1024
        ),
    )(tokens, cotangent, w_query, w_key, w_value, w_out)


def solution(mesh):
    placed = (P(("ctxa", "ctxb"), None), P(("ctxa", "ctxb"), None), P(), P(), P(), P())
    return jax.shard_map(
        shards, mesh=mesh, in_specs=placed, out_specs=P(("ctxa", "ctxb"), None), check_vma=False
    )
```

```python
import functools
import math

import jax
import jax.numpy as jnp
from jax import lax
from jax.experimental import pallas as pl
from jax.experimental.pallas import tpu as pltpu
from jax.sharding import PartitionSpec as P

MESH = pl.DeviceIdType.MESH
F32 = jnp.float32
BF16 = jnp.bfloat16

DH = 128
PAIR = 2 * DH
PAIRS = 4
SUB = 256
PARTS = 4
NY = 4
NZ = 4
NA = 8
ROWS = DH // NY
DEPTH = 512
CHUNK = 512
KEYS, GRADS = 0, PAIRS


K, G = KEYS, GRADS
ORDER = (
    ("got", 4), ("kv", 1), ("ks", 0),
    ("got", 5), ("get", 8), ("ys", K), ("kv", 2), ("ks", 1),
    ("got", 6), ("get", 9), ("ys", K + 1), ("kv", 3), ("ks", 2),
    ("got", 7), ("get", 10), ("ys", K + 2), ("qg", 0), ("ks", 3),
    ("got", 8), ("ys", K + 3), ("yf", K), ("zs", K), ("qg", 1), ("gs", 0),
    ("got", 9), ("ys", G), ("yf", K + 1), ("zs", K + 1), ("qg", 2), ("gs", 1),
    ("got", 10), ("ys", G + 1), ("yf", K + 2), ("zs", K + 2), ("zf", K), ("xs", K), ("qg", 3), ("gs", 2), ("gs", 3),
    ("ys", G + 2), ("ys", G + 3), ("yf", K + 3), ("zs", K + 3), ("zf", K + 1), ("xs", K + 1), ("yf", G), ("zs", G), ("a", 0),
    ("zf", K + 2), ("xs", K + 2), ("yf", G + 1), ("zs", G + 1), ("a", 1),
    ("xf", K), ("bs", K), ("zf", K + 3), ("xs", K + 3), ("a", 2),
    ("xf", K + 1), ("bs", K + 1), ("yf", G + 2), ("zs", G + 2), ("yf", G + 3), ("zs", G + 3), ("zf", G), ("xs", G), ("a", 3),
    ("zf", G + 1), ("xs", G + 1), ("xf", K + 2), ("bs", K + 2), ("bf", K), ("bq", 0), ("pq", 0),
    ("xf", K + 3), ("bs", K + 3), ("zf", G + 2), ("xs", G + 2), ("bf", K + 1), ("bq", 1), ("pq", 1),
    ("zf", G + 3), ("xs", G + 3), ("xf", G), ("bs", G), ("bf", K + 2), ("bq", 2), ("pq", 2),
    ("xf", G + 1), ("bs", G + 1), ("bf", K + 3), ("bq", 3), ("pq", 3),
    ("xf", G + 2), ("bs", G + 2), ("bf", G), ("br", 0), ("xf", G + 3), ("bs", G + 3), ("pr", 0),
    ("bf", G + 1), ("br", 1), ("pr", 1),
    ("bf", G + 2), ("br", 2), ("pr", 2),
    ("bf", G + 3), ("br", 3), ("pr", 3),
)


def dot(left, right, left_dim=1, right_dim=0):
    return lax.dot_general(
        left, right, (((left_dim,), (right_dim,)), ((), ())), preferred_element_type=F32
    )


def diagonal(first, second):
    zero = jnp.zeros_like(first)
    return jnp.concatenate(
        [jnp.concatenate([first, zero], axis=1), jnp.concatenate([zero, second], axis=1)], axis=0
    )


def kernel(
    factor,
    tok_h, cot_h, wq_h, wk_h, wv_h, wo_h, out,
    tok, cot, wall, wo, qkvg, intra, grads, acc,
    local, sbuf, ybuf, zbuf, xown, xbuf, back, pre,
    load_sem,
    y_send, y_recv, z_send, z_recv, x_send, x_recv, b_send, b_recv,
):
    a = lax.axis_index("ctxa")
    b = lax.axis_index("ctxb")
    z, y = b // NY, b % NY

    def y_peer(step):
        return (a, z * NY + (y + step) % NY)

    def z_peer(step):
        return (a, ((z + step) % NZ) * NY + y)

    def x_peer(step):
        return ((a + step) % NA, b)

    barrier = pltpu.get_barrier_semaphore()
    peers = [y_peer(s) for s in range(1, NY)]
    peers += [z_peer(s) for s in range(1, NZ)]
    peers += [x_peer(s) for s in range(1, NA)]

    def columns(p, which, count=1):
        first = p if which == 0 else PAIRS + 2 * p + which - 1
        return slice(first * PAIR, (first + count) * PAIR)

    def take(ref, sem):
        pltpu.make_async_copy(ref, ref, sem).wait()

    def part(n):
        return slice(n * DEPTH, (n + 1) * DEPTH)

    def weight(p, which, rows=slice(None), sem=None):
        sem = load_sem.at[4 * p + which if sem is None else sem]
        cols = slice(p * PAIR, (p + 1) * PAIR)
        if which == 3:
            return pltpu.make_async_copy(wo_h.at[cols, :], wo.at[cols, :], sem)
        source = (wq_h, wk_h, wv_h)[which]
        return pltpu.make_async_copy(source.at[rows, cols], wall.at[rows, columns(p, which)], sem)

    first = 4 * PAIRS
    loads = []
    for n in range(PARTS):
        token = pltpu.make_async_copy(
            tok_h.at[:, part(n)], tok.at[:, part(n)], load_sem.at[first + 2 * n]
        )
        loads += [[token, *[weight(0, which, part(n), first + 2 * n + 1) for which in (1, 2)]]]
    loads += [[weight(p, 1, sem=4 * p + 1), weight(p, 2, sem=4 * p + 1)] for p in range(1, PAIRS)]
    load_cot = pltpu.make_async_copy(cot_h, cot, load_sem.at[2])
    loads += [[load_cot, weight(0, 0, sem=0), weight(0, 3)]]
    loads += [[weight(p, 0), weight(p, 3)] for p in range(1, PAIRS)]

    def fetch(group):
        for load in loads[group]:
            load.start()

    def arrive(group):
        if group < PARTS:
            take(tok.at[:, part(group)], load_sem.at[first + 2 * group])
            take(wall.at[part(group), columns(0, 1, 2)], load_sem.at[first + 2 * group + 1])
        elif group < PARTS + PAIRS - 1:
            p = group - PARTS + 1
            take(wall.at[:, columns(p, 1, 2)], load_sem.at[4 * p + 1])
        else:
            for load in loads[group]:
                load.wait()

    def remote(source, target, sent, received, device):
        return pltpu.make_async_remote_copy(
            src_ref=source, dst_ref=target, send_sem=sent, recv_sem=received,
            device_id=device, device_id_type=MESH,
        )

    def y_copy(m, step):
        return remote(
            sbuf.at[m, :, (y + step) % NY], ybuf.at[m, y],
            y_send.at[0], y_recv.at[m], y_peer(step),
        )

    def z_copy(m, step):
        return remote(
            zbuf.at[m, z], zbuf.at[m, z],
            z_send.at[0], z_recv.at[m], z_peer(step),
        )

    def x_copy(m, step):
        return remote(
            xown.at[m], xbuf.at[m, a],
            x_send.at[0], x_recv.at[m], x_peer(step if m < GRADS else NA - step),
        )

    def b_copy(m, step):
        return remote(
            back.at[m, (y + step) % NY], pre.at[m, :, y],
            b_send.at[0], b_recv.at[m], y_peer(step),
        )

    def start(copy, count, m):
        for step in range(1, count):
            copy(m, step).start()

    def start_y(m):
        start(y_copy, NY, m)

    def start_z(m):
        start(z_copy, NZ, m)

    def start_x(m):
        for step in range(1, NA):
            pl.when(a + step < NA if m < GRADS else a >= step)(x_copy(m, step).start)

    def start_b(m):
        start(b_copy, NY, m)

    def finish_y(m):
        take(ybuf.at[m, 1:], y_recv.at[m])
        ybuf[m, y] = sbuf[m, :, y]
        total = ybuf[m, 0].astype(F32)
        for at in range(1, NY):
            total = total + ybuf[m, at].astype(F32)
        zbuf[m, z] = total.astype(BF16)

    def finish_z(m):
        take(zbuf.at[m, 1:], z_recv.at[m])
        total = zbuf[m, 0].astype(F32)
        for at in range(1, NZ):
            total = total + zbuf[m, at].astype(F32)
        xown[m] = total.astype(BF16)

    def finish_x(m):
        keys = m < GRADS
        for count in range(1, NA):
            pl.when(a == (count if keys else NA - 1 - count))(
                functools.partial(take, xbuf.at[m, :count], x_recv.at[m])
            )
        total = jnp.zeros((2, ROWS, DH), F32)
        for at in range(NA):
            total = total + jnp.where(at < a if keys else at > a, xbuf[m, at].astype(F32), 0.0)
        for at in range(NZ):
            total = total + jnp.where(at < z if keys else at > z, zbuf[m, at].astype(F32), 0.0)
        for at in range(NY) if keys else reversed(range(NY)):
            back[m, at] = total.astype(BF16)
            total = total + ybuf[m, at].astype(F32)
        pre[m, :, y] = back[m, y]

    def finish_b(m):
        take(pre.at[m, :, 1:], b_recv.at[m])

    def states(p, kind):
        left, right = (1, 2) if kind == 0 else (0, 3)
        m = kind * PAIRS + p
        for head in range(2):
            cols = slice(head * DH, (head + 1) * DH)
            parts = [
                dot(qkvg[p, left, rows, cols], qkvg[p, right, rows, cols], 0, 0)
                for rows in (slice(0, SUB), slice(SUB, 2 * SUB))
            ]
            local[m, head] = parts[kind]
            sbuf[m, head] = (parts[0] + parts[1]).astype(BF16).reshape(NY, ROWS, DH)

    def keep_keys_values(p, both):
        both = both.astype(BF16)
        qkvg[p, 1] = both[:, :PAIR]
        qkvg[p, 2] = both[:, PAIR:]

    def first_keys_values():
        total = 0.0
        for n in range(PARTS):
            arrive(n)
            fetch(n + PARTS)
            total = total + dot(tok[:, part(n)], wall[part(n), columns(0, 1, 2)])
        keep_keys_values(0, total)

    def keys_values(p):
        keep_keys_values(p, dot(tok[...], wall[:, columns(p, 1, 2)]))

    def query_grad(p):
        qkvg[p, 0] = dot(tok[...], wall[:, columns(p, 0)]).astype(BF16)
        qkvg[p, 3] = dot(cot[...], wo[p * PAIR : (p + 1) * PAIR], 1, 1).astype(BF16)

    down = lax.broadcasted_iota(jnp.int32, (SUB, SUB), 0)
    across = lax.broadcasted_iota(jnp.int32, (SUB, SUB), 1)
    lower, upper = down >= across, across >= down

    def attention(p):
        for block in range(2):
            for head in range(2):
                cols = slice(head * DH, (head + 1) * DH)
                rows = slice(block * SUB, (block + 1) * SUB)
                query, keys = qkvg[p, 0, rows, cols], qkvg[p, 1, rows, cols]
                values, grad_out = qkvg[p, 2, rows, cols], qkvg[p, 3, rows, cols]
                probe = jnp.where(lower, dot(grad_out, values, 1, 1), 0.0).astype(BF16)
                probe_t = jnp.where(upper, dot(values, grad_out, 1, 1), 0.0).astype(BF16)
                attend_t = jnp.where(upper, dot(keys, query, 1, 1), 0.0).astype(BF16)
                intra[p, 0, rows, cols] = dot(probe, keys)
                intra[p, 1, rows, cols] = dot(probe_t, query)
                intra[p, 2, rows, cols] = dot(attend_t, grad_out)

    def moved(m, block):
        whole = [pre[m, head].reshape(DH, DH) for head in range(2)]
        if block == (1 if m < GRADS else 0):
            whole = [(whole[head].astype(F32) + local[m, head]).astype(BF16) for head in range(2)]
        return diagonal(*whole)

    def finish(p, which, rows, term):
        grads[rows, columns(p, which)] = (factor * (intra[p, which, rows] + term)).astype(BF16)

    def between_query(p):
        for block in range(2):
            rows = slice(block * SUB, (block + 1) * SUB)
            finish(p, 0, rows, dot(qkvg[p, 3, rows], moved(KEYS + p, block), 1, 1))

    def between_rest(p):
        for block in range(2):
            rows = slice(block * SUB, (block + 1) * SUB)
            after = moved(GRADS + p, block)
            finish(p, 1, rows, dot(qkvg[p, 2, rows], after, 1, 1))
            finish(p, 2, rows, dot(qkvg[p, 1, rows], after, 1, 0))

    def product(cols, first=False, last=False):
        for n in range(acc.shape[0]):
            rows = slice(n * CHUNK, (n + 1) * CHUNK)
            part = dot(grads[:, cols], wall[rows, cols], 1, 1)
            part = part if first else acc[n] + part
            if last:
                out[:, rows] = part.astype(BF16)
            else:
                acc[n] = part

    blocks = {
        "kv": keys_values, "qg": query_grad, "ks": lambda p: states(p, 0), "gs": lambda p: states(p, 1), "a": attention, "bq": between_query, "br": between_rest,
        "yf": finish_y, "zf": finish_z, "xf": finish_x, "bf": finish_b,
        "ys": start_y, "zs": start_z, "xs": start_x, "bs": start_b,
        "get": fetch, "got": arrive,
        "pq": lambda p: product(columns(p, 0), first=p == 0),
        "pr": lambda p: product(columns(p, 1, 2), last=p == PAIRS - 1),
    }

    for n in range(PARTS):
        fetch(n)
    for peer in peers:
        pl.semaphore_signal(barrier, inc=1, device_id=peer, device_id_type=MESH)
    first_keys_values()
    pl.semaphore_wait(barrier, len(peers))
    for name, at in ORDER:
        blocks[name](at)

    take(ybuf.at[:, 1:], y_send.at[0])
    take(zbuf.at[:, 1:], z_send.at[0])
    take(xbuf.at[:PAIRS, 1:], x_send.at[0])
    take(back.at[:, 1:], b_send.at[0])


def shards(tokens, cotangent, w_query, w_key, w_value, w_out):
    rows, width = tokens.shape
    blocks = lax.axis_size("ctxa") * lax.axis_size("ctxb")
    factor = 1.0 / math.sqrt(DH * rows * blocks)
    slot = (2, ROWS, DH)
    messages = 2 * PAIRS
    dma = pltpu.SemaphoreType.DMA
    return pl.pallas_call(
        functools.partial(kernel, factor),
        out_shape=pltpu.VMEM((rows, width), BF16),
        in_specs=[pl.BlockSpec(memory_space=pl.ANY)] * 6,
        out_specs=pl.BlockSpec(memory_space=pltpu.VMEM),
        scratch_shapes=[
            pltpu.VMEM((rows, width), BF16),
            pltpu.VMEM((rows, width), BF16),
            pltpu.VMEM((width, 3 * PAIRS * PAIR), BF16),
            pltpu.VMEM((PAIRS * PAIR, width), BF16),
            pltpu.VMEM((PAIRS, 4, rows, PAIR), BF16),
            pltpu.VMEM((PAIRS, 3, rows, PAIR), F32),
            pltpu.VMEM((rows, 3 * PAIRS * PAIR), BF16),
            pltpu.VMEM((width // CHUNK, rows, CHUNK), F32),
            pltpu.VMEM((messages, 2, DH, DH), F32),
            pltpu.VMEM((messages, 2, NY, ROWS, DH), BF16),
            pltpu.VMEM((messages, NY, *slot), BF16),
            pltpu.VMEM((messages, NZ, *slot), BF16),
            pltpu.VMEM((messages, *slot), BF16),
            pltpu.VMEM((messages, NA, *slot), BF16),
            pltpu.VMEM((messages, NY, *slot), BF16),
            pltpu.VMEM((messages, 2, NY, ROWS, DH), BF16),
            dma((4 * PAIRS + 2 * PARTS,)),
            *[dma((1,)), dma((messages,))] * 4,
        ],
        compiler_params=pltpu.CompilerParams(
            collective_id=0, has_side_effects=True, vmem_limit_bytes=56 * 1024 * 1024
        ),
    )(tokens, cotangent, w_query, w_key, w_value, w_out)


def solution(mesh):
    placed = (P(("ctxa", "ctxb"), None), P(("ctxa", "ctxb"), None), P(), P(), P(), P())
    return jax.shard_map(
        shards, mesh=mesh, in_specs=placed, out_specs=P(("ctxa", "ctxb"), None), check_vma=False
    )
```

```python
import functools
import math

import jax
import jax.numpy as jnp
from jax import lax
from jax.experimental import pallas as pl
from jax.experimental.pallas import tpu as pltpu
from jax.sharding import PartitionSpec as P

MESH = pl.DeviceIdType.MESH
F32 = jnp.float32
BF16 = jnp.bfloat16

DH = 128
PAIR = 2 * DH
PAIRS = 4
SUB = 256
PARTS = 4
NX = 4
NY = 4
NZ = 4
NG = 2 * NY
ROWS = DH // NG
DEPTH = 512
CHUNK = 512
KEYS, GRADS = 0, PAIRS


K, G = KEYS, GRADS
FIRST = (4, 7, 5, 8)
ORDER = (
    ("got", 4), ("kv", 1), ("ks", 0),
    ("got", 7), ("get", 6), ("ys", K), ("qg", 0), ("ks", 1),
    ("got", 5), ("get", 9), ("ys", K + 1), ("kv", 2), ("gs", 0),
    ("got", 8), ("get", 10), ("ys", G), ("qg", 1), ("ks", 2),
    ("got", 6), ("ys", K + 2), ("yf", K), ("zs", K), ("kv", 3), ("gs", 1),
    ("got", 9), ("ys", G + 1), ("yf", K + 1), ("zs", K + 1), ("qg", 2), ("ks", 3),
    ("got", 10), ("ys", K + 3), ("yf", G), ("zs", G), ("qg", 3), ("gs", 2), ("gs", 3),
    ("ys", G + 2), ("ys", G + 3), ("zf", K), ("xs", K), ("zf", K + 1), ("xs", K + 1), ("yf", K + 2), ("zs", K + 2), ("yf", G + 1), ("zs", G + 1), ("a", 0),
    ("zf", G), ("xs", G), ("a", 1),
    ("xf", K), ("bs", K), ("yf", K + 3), ("zs", K + 3), ("a", 2),
    ("xf", K + 1), ("bs", K + 1), ("zf", K + 2), ("xs", K + 2), ("zf", G + 1), ("xs", G + 1), ("yf", G + 2), ("zs", G + 2), ("yf", G + 3), ("zs", G + 3), ("a", 3),
    ("xf", G), ("bs", G), ("zf", K + 3), ("xs", K + 3), ("bf", K), ("bq", 0),
    ("xf", K + 2), ("bs", K + 2), ("xf", G + 1), ("bs", G + 1), ("pq", 0),
    ("zf", G + 2), ("xs", G + 2), ("bf", K + 1), ("bq", 1),
    ("pq", 1),
    ("zf", G + 3), ("xs", G + 3), ("bf", G), ("br", 0),
    ("xf", K + 3), ("bs", K + 3), ("pr", 0),
    ("xf", G + 2), ("bs", G + 2), ("bf", K + 2), ("bq", 2),
    ("pq", 2),
    ("bf", G + 1), ("br", 1),
    ("xf", G + 3), ("bs", G + 3), ("pr", 1),
    ("bf", K + 3), ("bq", 3),
    ("pq", 3),
    ("bf", G + 2), ("br", 2),
    ("pr", 2),
    ("bf", G + 3), ("br", 3),
    ("pr", 3),
)


def dot(left, right, left_dim=1, right_dim=0):
    return lax.dot_general(
        left, right, (((left_dim,), (right_dim,)), ((), ())), preferred_element_type=F32
    )


def diagonal(first, second):
    zero = jnp.zeros_like(first)
    return jnp.concatenate(
        [jnp.concatenate([first, zero], axis=1), jnp.concatenate([zero, second], axis=1)], axis=0
    )


def kernel(
    factor,
    tok_h, cot_h, wq_h, wk_h, wv_h, wo_h, out,
    tok, cot, wall, wo, qkvg, intra, grads, acc,
    local, sbuf, ybuf, zbuf, xown, xbuf, back, pre,
    load_sem,
    y_send, y_recv, z_send, z_recv, x_send, x_recv, b_send, b_recv,
):
    a = lax.axis_index("ctxa")
    b = lax.axis_index("ctxb")
    x, core = a // 2, a % 2
    z, y = b // NY, b % NY
    g = core * NY + y

    def g_peer(step):
        at = (g + step) % NG
        return (2 * x + at // NY, z * NY + at % NY)

    def z_peer(step):
        return (a, ((z + step) % NZ) * NY + y)

    def x_peer(step):
        return (2 * ((x + step) % NX) + core, b)

    barrier = pltpu.get_barrier_semaphore()
    peers = [g_peer(s) for s in range(1, NG)]
    peers += [z_peer(s) for s in range(1, NZ)]
    peers += [x_peer(s) for s in range(1, NX)]

    def columns(p, which, count=1):
        first = p if which == 0 else PAIRS + 2 * p + which - 1
        return slice(first * PAIR, (first + count) * PAIR)

    def take(ref, sem):
        pltpu.make_async_copy(ref, ref, sem).wait()

    def part(n):
        return slice(n * DEPTH, (n + 1) * DEPTH)

    def weight(p, which, rows=slice(None), sem=None):
        sem = load_sem.at[4 * p + which if sem is None else sem]
        cols = slice(p * PAIR, (p + 1) * PAIR)
        if which == 3:
            return pltpu.make_async_copy(wo_h.at[cols, :], wo.at[cols, :], sem)
        source = (wq_h, wk_h, wv_h)[which]
        return pltpu.make_async_copy(source.at[rows, cols], wall.at[rows, columns(p, which)], sem)

    first = 4 * PAIRS
    loads = []
    for n in range(PARTS):
        token = pltpu.make_async_copy(
            tok_h.at[:, part(n)], tok.at[:, part(n)], load_sem.at[first + 2 * n]
        )
        loads += [[token, *[weight(0, which, part(n), first + 2 * n + 1) for which in (1, 2)]]]
    loads += [[weight(p, 1, sem=4 * p + 1), weight(p, 2, sem=4 * p + 1)] for p in range(1, PAIRS)]
    load_cot = pltpu.make_async_copy(cot_h, cot, load_sem.at[2])
    loads += [[load_cot, weight(0, 0, sem=0), weight(0, 3)]]
    loads += [[weight(p, 0), weight(p, 3)] for p in range(1, PAIRS)]

    def fetch(group):
        for load in loads[group]:
            load.start()

    def arrive(group):
        if group < PARTS:
            take(tok.at[:, part(group)], load_sem.at[first + 2 * group])
            take(wall.at[part(group), columns(0, 1, 2)], load_sem.at[first + 2 * group + 1])
        elif group < PARTS + PAIRS - 1:
            p = group - PARTS + 1
            take(wall.at[:, columns(p, 1, 2)], load_sem.at[4 * p + 1])
        else:
            for load in loads[group]:
                load.wait()

    def remote(source, target, sent, received, device):
        return pltpu.make_async_remote_copy(
            src_ref=source, dst_ref=target, send_sem=sent, recv_sem=received,
            device_id=device, device_id_type=MESH,
        )

    def y_copy(m, step):
        return remote(
            sbuf.at[m, :, (g + step) % NG], ybuf.at[m, g],
            y_send.at[0], y_recv.at[m], g_peer(step),
        )

    def z_copy(m, step):
        return remote(
            zbuf.at[m, z], zbuf.at[m, z],
            z_send.at[0], z_recv.at[m], z_peer(step),
        )

    def x_copy(m, step):
        return remote(
            xown.at[m], xbuf.at[m, x],
            x_send.at[0], x_recv.at[m], x_peer(step if m < GRADS else NX - step),
        )

    def b_copy(m, step):
        return remote(
            back.at[m, (g + step) % NG], pre.at[m, :, g],
            b_send.at[0], b_recv.at[m], g_peer(step),
        )

    def start(copy, count, m):
        for step in range(1, count):
            copy(m, step).start()

    def start_y(m):
        start(y_copy, NG, m)

    def start_z(m):
        start(z_copy, NZ, m)

    def start_x(m):
        for step in range(1, NX):
            pl.when(x + step < NX if m < GRADS else x >= step)(x_copy(m, step).start)

    def start_b(m):
        start(b_copy, NG, m)

    def sum_of(parts):
        return functools.reduce(lambda total, part: total + part, parts)

    def finish_y(m):
        take(ybuf.at[m, 1:], y_recv.at[m])
        ybuf[m, g] = sbuf[m, :, g]
        for half in range(2):
            line = range(half * NY, (half + 1) * NY)
            zbuf[m, z, half] = sum_of(ybuf[m, at].astype(F32) for at in line).astype(BF16)

    def finish_z(m):
        take(zbuf.at[m, 1:], z_recv.at[m])
        both = sum_of(zbuf[m, at].astype(F32) for at in range(NZ))
        xown[m] = (both[0] + both[1]).astype(BF16)

    def finish_x(m):
        keys = m < GRADS
        for count in range(1, NX):
            pl.when(x == (count if keys else NX - 1 - count))(
                functools.partial(take, xbuf.at[m, :count], x_recv.at[m])
            )
        outer = sum_of(
            jnp.where(at < x if keys else at > x, xbuf[m, at].astype(F32), 0.0) for at in range(NX)
        )
        for half in (0, 1) if keys else (1, 0):
            planes = [zbuf[m, at, half].astype(F32) for at in range(NZ)]
            total = outer + sum_of(
                jnp.where(at < z if keys else at > z, planes[at], 0.0) for at in range(NZ)
            )
            outer = outer + sum_of(planes)
            line = range(half * NY, (half + 1) * NY)
            for at in line if keys else reversed(line):
                back[m, at] = total.astype(BF16)
                total = total + ybuf[m, at].astype(F32)
        pre[m, :, g] = back[m, g]

    def finish_b(m):
        take(pre.at[m, :, 1:], b_recv.at[m])

    def states(p, kind):
        left, right = (1, 2) if kind == 0 else (0, 3)
        m = kind * PAIRS + p
        for head in range(2):
            cols = slice(head * DH, (head + 1) * DH)
            parts = [
                dot(qkvg[p, left, rows, cols], qkvg[p, right, rows, cols], 0, 0)
                for rows in (slice(0, SUB), slice(SUB, 2 * SUB))
            ]
            local[m, head] = parts[kind]
            sbuf[m, head] = (parts[0] + parts[1]).astype(BF16).reshape(NG, ROWS, DH)

    def keep_keys_values(p, both):
        both = both.astype(BF16)
        qkvg[p, 1] = both[:, :PAIR]
        qkvg[p, 2] = both[:, PAIR:]

    def first_keys_values():
        total = 0.0
        for n in range(PARTS):
            arrive(n)
            fetch(FIRST[n])
            total = total + dot(tok[:, part(n)], wall[part(n), columns(0, 1, 2)])
        keep_keys_values(0, total)

    def keys_values(p):
        keep_keys_values(p, dot(tok[...], wall[:, columns(p, 1, 2)]))

    def query_grad(p):
        qkvg[p, 0] = dot(tok[...], wall[:, columns(p, 0)]).astype(BF16)
        qkvg[p, 3] = dot(cot[...], wo[p * PAIR : (p + 1) * PAIR], 1, 1).astype(BF16)

    down = lax.broadcasted_iota(jnp.int32, (SUB, SUB), 0)
    across = lax.broadcasted_iota(jnp.int32, (SUB, SUB), 1)
    lower, upper = down >= across, across >= down

    def attention(p):
        for block in range(2):
            for head in range(2):
                cols = slice(head * DH, (head + 1) * DH)
                rows = slice(block * SUB, (block + 1) * SUB)
                query, keys = qkvg[p, 0, rows, cols], qkvg[p, 1, rows, cols]
                values, grad_out = qkvg[p, 2, rows, cols], qkvg[p, 3, rows, cols]
                probe = jnp.where(lower, dot(grad_out, values, 1, 1), 0.0).astype(BF16)
                probe_t = jnp.where(upper, dot(values, grad_out, 1, 1), 0.0).astype(BF16)
                attend_t = jnp.where(upper, dot(keys, query, 1, 1), 0.0).astype(BF16)
                intra[p, 0, rows, cols] = dot(probe, keys)
                intra[p, 1, rows, cols] = dot(probe_t, query)
                intra[p, 2, rows, cols] = dot(attend_t, grad_out)

    def moved(m, block):
        whole = [pre[m, head].reshape(DH, DH) for head in range(2)]
        if block == (1 if m < GRADS else 0):
            whole = [(whole[head].astype(F32) + local[m, head]).astype(BF16) for head in range(2)]
        return diagonal(*whole)

    def finish(p, which, rows, term):
        grads[rows, columns(p, which)] = (factor * (intra[p, which, rows] + term)).astype(BF16)

    def between_query(p):
        for block in range(2):
            rows = slice(block * SUB, (block + 1) * SUB)
            finish(p, 0, rows, dot(qkvg[p, 3, rows], moved(KEYS + p, block), 1, 1))

    def between_rest(p):
        for block in range(2):
            rows = slice(block * SUB, (block + 1) * SUB)
            after = moved(GRADS + p, block)
            finish(p, 1, rows, dot(qkvg[p, 2, rows], after, 1, 1))
            finish(p, 2, rows, dot(qkvg[p, 1, rows], after, 1, 0))

    def product(cols, first=False, last=False):
        for n in range(acc.shape[0]):
            rows = slice(n * CHUNK, (n + 1) * CHUNK)
            part = dot(grads[:, cols], wall[rows, cols], 1, 1)
            part = part if first else acc[n] + part
            if last:
                out[:, rows] = part.astype(BF16)
            else:
                acc[n] = part

    blocks = {
        "kv": keys_values, "qg": query_grad, "ks": lambda p: states(p, 0), "gs": lambda p: states(p, 1), "a": attention, "bq": between_query, "br": between_rest,
        "yf": finish_y, "zf": finish_z, "xf": finish_x, "bf": finish_b,
        "ys": start_y, "zs": start_z, "xs": start_x, "bs": start_b,
        "get": fetch, "got": arrive,
        "pq": lambda p: product(columns(p, 0), first=p == 0),
        "pr": lambda p: product(columns(p, 1, 2), last=p == PAIRS - 1),
    }

    for n in range(PARTS):
        fetch(n)
    for peer in peers:
        pl.semaphore_signal(barrier, inc=1, device_id=peer, device_id_type=MESH)
    first_keys_values()
    pl.semaphore_wait(barrier, len(peers))
    for name, at in ORDER:
        blocks[name](at)

    take(ybuf.at[:, 1:], y_send.at[0])
    take(zbuf.at[:, 1:], z_send.at[0])
    take(xbuf.at[:PAIRS, 1:], x_send.at[0])
    take(back.at[:, 1:], b_send.at[0])


def shards(tokens, cotangent, w_query, w_key, w_value, w_out):
    rows, width = tokens.shape
    blocks = lax.axis_size("ctxa") * lax.axis_size("ctxb")
    factor = 1.0 / math.sqrt(DH * rows * blocks)
    slot = (2, ROWS, DH)
    messages = 2 * PAIRS
    dma = pltpu.SemaphoreType.DMA
    return pl.pallas_call(
        functools.partial(kernel, factor),
        out_shape=pltpu.VMEM((rows, width), BF16),
        in_specs=[pl.BlockSpec(memory_space=pl.ANY)] * 6,
        out_specs=pl.BlockSpec(memory_space=pltpu.VMEM),
        scratch_shapes=[
            pltpu.VMEM((rows, width), BF16),
            pltpu.VMEM((rows, width), BF16),
            pltpu.VMEM((width, 3 * PAIRS * PAIR), BF16),
            pltpu.VMEM((PAIRS * PAIR, width), BF16),
            pltpu.VMEM((PAIRS, 4, rows, PAIR), BF16),
            pltpu.VMEM((PAIRS, 3, rows, PAIR), F32),
            pltpu.VMEM((rows, 3 * PAIRS * PAIR), BF16),
            pltpu.VMEM((width // CHUNK, rows, CHUNK), F32),
            pltpu.VMEM((messages, 2, DH, DH), F32),
            pltpu.VMEM((messages, 2, NG, ROWS, DH), BF16),
            pltpu.VMEM((messages, NG, *slot), BF16),
            pltpu.VMEM((messages, NZ, 2, *slot), BF16),
            pltpu.VMEM((messages, *slot), BF16),
            pltpu.VMEM((messages, NX, *slot), BF16),
            pltpu.VMEM((messages, NG, *slot), BF16),
            pltpu.VMEM((messages, 2, NG, ROWS, DH), BF16),
            dma((4 * PAIRS + 2 * PARTS,)),
            *[dma((1,)), dma((messages,))] * 4,
        ],
        compiler_params=pltpu.CompilerParams(
            collective_id=0, has_side_effects=True, vmem_limit_bytes=56 * 1024 * 1024
        ),
    )(tokens, cotangent, w_query, w_key, w_value, w_out)


def solution(mesh):
    placed = (P(("ctxa", "ctxb"), None), P(("ctxa", "ctxb"), None), P(), P(), P(), P())
    return jax.shard_map(
        shards, mesh=mesh, in_specs=placed, out_specs=P(("ctxa", "ctxb"), None), check_vma=False
    )
```

```python
import functools
import math

import jax
import jax.numpy as jnp
from jax import lax
from jax.experimental import pallas as pl
from jax.experimental.pallas import tpu as pltpu
from jax.sharding import PartitionSpec as P

MESH = pl.DeviceIdType.MESH
F32 = jnp.float32
BF16 = jnp.bfloat16

DH = 128
PAIR = 2 * DH
PAIRS = 4
SUB = 256
PARTS = 4
NX = 4
NY = 4
NZ = 4
NG = 2 * NY
ROWS = DH // NG
DEPTH = 512
CHUNK = 512
KEYS, GRADS = 0, PAIRS


K, G = KEYS, GRADS
FIRST = (4, 7, 5, 8)
ORDER = (
    ("got", 4), ("kv", 1), ("ks", 0),
    ("got", 7), ("get", 6), ("ys", K), ("qg", 0), ("ks", 1),
    ("got", 5), ("get", 9), ("ys", K + 1), ("kv", 2), ("gs", 0),
    ("got", 8), ("get", 10), ("ys", G), ("qg", 1), ("ks", 2),
    ("got", 6), ("ys", K + 2), ("yf", K), ("zs", K), ("kv", 3), ("gs", 1),
    ("got", 9), ("ys", G + 1), ("yf", K + 1), ("zs", K + 1), ("qg", 2), ("ks", 3),
    ("got", 10), ("ys", K + 3), ("yf", G), ("zs", G), ("qg", 3), ("gs", 2), ("gs", 3),
    ("ys", G + 2), ("ys", G + 3), ("zf", K), ("xs", K), ("zf", K + 1), ("xs", K + 1), ("yf", K + 2), ("zs", K + 2), ("yf", G + 1), ("zs", G + 1), ("a", 0),
    ("zf", G), ("xs", G), ("a", 1),
    ("xf", K), ("bs", K), ("yf", K + 3), ("zs", K + 3), ("a", 2),
    ("xf", K + 1), ("bs", K + 1), ("zf", K + 2), ("xs", K + 2), ("zf", G + 1), ("xs", G + 1), ("yf", G + 2), ("zs", G + 2), ("yf", G + 3), ("zs", G + 3), ("a", 3),
    ("xf", G), ("bs", G), ("zf", K + 3), ("xs", K + 3), ("bf", K), ("bq", 0),
    ("xf", K + 2), ("bs", K + 2), ("xf", G + 1), ("bs", G + 1), ("pq", 0),
    ("zf", G + 2), ("xs", G + 2), ("bf", K + 1), ("bq", 1),
    ("pq", 1),
    ("zf", G + 3), ("xs", G + 3), ("bf", G), ("br", 0),
    ("xf", K + 3), ("bs", K + 3), ("pr", 0),
    ("xf", G + 2), ("bs", G + 2), ("bf", K + 2), ("bq", 2),
    ("pq", 2),
    ("bf", G + 1), ("br", 1),
    ("xf", G + 3), ("bs", G + 3), ("pr", 1),
    ("bf", K + 3), ("bq", 3),
    ("pq", 3),
    ("bf", G + 2), ("br", 2),
    ("pr", 2),
    ("bf", G + 3), ("br", 3),
)


def dot(left, right, left_dim=1, right_dim=0):
    return lax.dot_general(
        left, right, (((left_dim,), (right_dim,)), ((), ())), preferred_element_type=F32
    )


def diagonal(first, second):
    zero = jnp.zeros_like(first)
    return jnp.concatenate(
        [jnp.concatenate([first, zero], axis=1), jnp.concatenate([zero, second], axis=1)], axis=0
    )


def kernel(
    factor,
    tok_h, cot_h, wq_h, wk_h, wv_h, wo_h, acc, grads, wall,
    tok, cot, wo, qkvg, intra,
    local, sbuf, ybuf, zbuf, xown, xbuf, back, pre,
    load_sem,
    y_send, y_recv, z_send, z_recv, x_send, x_recv, b_send, b_recv,
):
    a = lax.axis_index("ctxa")
    b = lax.axis_index("ctxb")
    x, core = a // 2, a % 2
    z, y = b // NY, b % NY
    g = core * NY + y

    def g_peer(step):
        at = (g + step) % NG
        return (2 * x + at // NY, z * NY + at % NY)

    def z_peer(step):
        return (a, ((z + step) % NZ) * NY + y)

    def x_peer(step):
        return (2 * ((x + step) % NX) + core, b)

    barrier = pltpu.get_barrier_semaphore()
    peers = [g_peer(s) for s in range(1, NG)]
    peers += [z_peer(s) for s in range(1, NZ)]
    peers += [x_peer(s) for s in range(1, NX)]

    def columns(p, which, count=1):
        first = p if which == 0 else PAIRS + 2 * p + which - 1
        return slice(first * PAIR, (first + count) * PAIR)

    def take(ref, sem):
        pltpu.make_async_copy(ref, ref, sem).wait()

    def part(n):
        return slice(n * DEPTH, (n + 1) * DEPTH)

    def weight(p, which, rows=slice(None), sem=None):
        sem = load_sem.at[4 * p + which if sem is None else sem]
        cols = slice(p * PAIR, (p + 1) * PAIR)
        if which == 3:
            return pltpu.make_async_copy(wo_h.at[cols, :], wo.at[cols, :], sem)
        source = (wq_h, wk_h, wv_h)[which]
        return pltpu.make_async_copy(source.at[rows, cols], wall.at[rows, columns(p, which)], sem)

    first = 4 * PAIRS
    loads = []
    for n in range(PARTS):
        token = pltpu.make_async_copy(
            tok_h.at[:, part(n)], tok.at[:, part(n)], load_sem.at[first + 2 * n]
        )
        loads += [[token, *[weight(0, which, part(n), first + 2 * n + 1) for which in (1, 2)]]]
    loads += [[weight(p, 1, sem=4 * p + 1), weight(p, 2, sem=4 * p + 1)] for p in range(1, PAIRS)]
    load_cot = pltpu.make_async_copy(cot_h, cot, load_sem.at[2])
    loads += [[load_cot, weight(0, 0, sem=0), weight(0, 3)]]
    loads += [[weight(p, 0), weight(p, 3)] for p in range(1, PAIRS)]

    def fetch(group):
        for load in loads[group]:
            load.start()

    def arrive(group):
        if group < PARTS:
            take(tok.at[:, part(group)], load_sem.at[first + 2 * group])
            take(wall.at[part(group), columns(0, 1, 2)], load_sem.at[first + 2 * group + 1])
        elif group < PARTS + PAIRS - 1:
            p = group - PARTS + 1
            take(wall.at[:, columns(p, 1, 2)], load_sem.at[4 * p + 1])
        else:
            for load in loads[group]:
                load.wait()

    def remote(source, target, sent, received, device):
        return pltpu.make_async_remote_copy(
            src_ref=source, dst_ref=target, send_sem=sent, recv_sem=received,
            device_id=device, device_id_type=MESH,
        )

    def y_copy(m, step):
        return remote(
            sbuf.at[m, :, (g + step) % NG], ybuf.at[m, g],
            y_send.at[0], y_recv.at[m], g_peer(step),
        )

    def z_copy(m, step):
        return remote(
            zbuf.at[m, z], zbuf.at[m, z],
            z_send.at[0], z_recv.at[m], z_peer(step),
        )

    def x_copy(m, step):
        return remote(
            xown.at[m], xbuf.at[m, x],
            x_send.at[0], x_recv.at[m], x_peer(step if m < GRADS else NX - step),
        )

    def b_copy(m, step):
        return remote(
            back.at[m, (g + step) % NG], pre.at[m, :, g],
            b_send.at[0], b_recv.at[m], g_peer(step),
        )

    def start(copy, count, m):
        for step in range(1, count):
            copy(m, step).start()

    def start_y(m):
        start(y_copy, NG, m)

    def start_z(m):
        start(z_copy, NZ, m)

    def start_x(m):
        for step in range(1, NX):
            pl.when(x + step < NX if m < GRADS else x >= step)(x_copy(m, step).start)

    def start_b(m):
        start(b_copy, NG, m)

    def sum_of(parts):
        return functools.reduce(lambda total, part: total + part, parts)

    def finish_y(m):
        take(ybuf.at[m, 1:], y_recv.at[m])
        ybuf[m, g] = sbuf[m, :, g]
        for half in range(2):
            line = range(half * NY, (half + 1) * NY)
            zbuf[m, z, half] = sum_of(ybuf[m, at].astype(F32) for at in line).astype(BF16)

    def finish_z(m):
        take(zbuf.at[m, 1:], z_recv.at[m])
        both = sum_of(zbuf[m, at].astype(F32) for at in range(NZ))
        xown[m] = (both[0] + both[1]).astype(BF16)

    def finish_x(m):
        keys = m < GRADS
        for count in range(1, NX):
            pl.when(x == (count if keys else NX - 1 - count))(
                functools.partial(take, xbuf.at[m, :count], x_recv.at[m])
            )
        outer = sum_of(
            jnp.where(at < x if keys else at > x, xbuf[m, at].astype(F32), 0.0) for at in range(NX)
        )
        for half in (0, 1) if keys else (1, 0):
            planes = [zbuf[m, at, half].astype(F32) for at in range(NZ)]
            total = outer + sum_of(
                jnp.where(at < z if keys else at > z, planes[at], 0.0) for at in range(NZ)
            )
            outer = outer + sum_of(planes)
            line = range(half * NY, (half + 1) * NY)
            for at in line if keys else reversed(line):
                back[m, at] = total.astype(BF16)
                total = total + ybuf[m, at].astype(F32)
        pre[m, :, g] = back[m, g]

    def finish_b(m):
        take(pre.at[m, :, 1:], b_recv.at[m])

    def states(p, kind):
        left, right = (1, 2) if kind == 0 else (0, 3)
        m = kind * PAIRS + p
        for head in range(2):
            cols = slice(head * DH, (head + 1) * DH)
            parts = [
                dot(qkvg[p, left, rows, cols], qkvg[p, right, rows, cols], 0, 0)
                for rows in (slice(0, SUB), slice(SUB, 2 * SUB))
            ]
            local[m, head] = parts[kind]
            sbuf[m, head] = (parts[0] + parts[1]).astype(BF16).reshape(NG, ROWS, DH)

    def keep_keys_values(p, both):
        both = both.astype(BF16)
        qkvg[p, 1] = both[:, :PAIR]
        qkvg[p, 2] = both[:, PAIR:]

    def first_keys_values():
        total = 0.0
        for n in range(PARTS):
            arrive(n)
            fetch(FIRST[n])
            total = total + dot(tok[:, part(n)], wall[part(n), columns(0, 1, 2)])
        keep_keys_values(0, total)

    def keys_values(p):
        keep_keys_values(p, dot(tok[...], wall[:, columns(p, 1, 2)]))

    def query_grad(p):
        qkvg[p, 0] = dot(tok[...], wall[:, columns(p, 0)]).astype(BF16)
        qkvg[p, 3] = dot(cot[...], wo[p * PAIR : (p + 1) * PAIR], 1, 1).astype(BF16)

    down = lax.broadcasted_iota(jnp.int32, (SUB, SUB), 0)
    across = lax.broadcasted_iota(jnp.int32, (SUB, SUB), 1)
    lower, upper = down >= across, across >= down

    def attention(p):
        for block in range(2):
            for head in range(2):
                cols = slice(head * DH, (head + 1) * DH)
                rows = slice(block * SUB, (block + 1) * SUB)
                query, keys = qkvg[p, 0, rows, cols], qkvg[p, 1, rows, cols]
                values, grad_out = qkvg[p, 2, rows, cols], qkvg[p, 3, rows, cols]
                probe = jnp.where(lower, dot(grad_out, values, 1, 1), 0.0).astype(BF16)
                probe_t = jnp.where(upper, dot(values, grad_out, 1, 1), 0.0).astype(BF16)
                attend_t = jnp.where(upper, dot(keys, query, 1, 1), 0.0).astype(BF16)
                intra[p, 0, rows, cols] = dot(probe, keys)
                intra[p, 1, rows, cols] = dot(probe_t, query)
                intra[p, 2, rows, cols] = dot(attend_t, grad_out)

    def moved(m, block):
        whole = [pre[m, head].reshape(DH, DH) for head in range(2)]
        if block == (1 if m < GRADS else 0):
            whole = [(whole[head].astype(F32) + local[m, head]).astype(BF16) for head in range(2)]
        return diagonal(*whole)

    def finish(p, which, rows, term):
        grads[rows, columns(p, which)] = (factor * (intra[p, which, rows] + term)).astype(BF16)

    def between_query(p):
        for block in range(2):
            rows = slice(block * SUB, (block + 1) * SUB)
            finish(p, 0, rows, dot(qkvg[p, 3, rows], moved(KEYS + p, block), 1, 1))

    def between_rest(p):
        for block in range(2):
            rows = slice(block * SUB, (block + 1) * SUB)
            after = moved(GRADS + p, block)
            finish(p, 1, rows, dot(qkvg[p, 2, rows], after, 1, 1))
            finish(p, 2, rows, dot(qkvg[p, 1, rows], after, 1, 0))

    def product(cols, first=False):
        for n in range(acc.shape[0]):
            rows = slice(n * CHUNK, (n + 1) * CHUNK)
            part = dot(grads[:, cols], wall[rows, cols], 1, 1)
            acc[n] = part if first else acc[n] + part

    blocks = {
        "kv": keys_values, "qg": query_grad, "ks": lambda p: states(p, 0), "gs": lambda p: states(p, 1), "a": attention, "bq": between_query, "br": between_rest,
        "yf": finish_y, "zf": finish_z, "xf": finish_x, "bf": finish_b,
        "ys": start_y, "zs": start_z, "xs": start_x, "bs": start_b,
        "get": fetch, "got": arrive,
        "pq": lambda p: product(columns(p, 0), first=p == 0),
        "pr": lambda p: product(columns(p, 1, 2)),
    }

    for n in range(PARTS):
        fetch(n)
    for peer in peers:
        pl.semaphore_signal(barrier, inc=1, device_id=peer, device_id_type=MESH)
    first_keys_values()
    pl.semaphore_wait(barrier, len(peers))
    for name, at in ORDER:
        blocks[name](at)

    take(ybuf.at[:, 1:], y_send.at[0])
    take(zbuf.at[:, 1:], z_send.at[0])
    take(xbuf.at[:PAIRS, 1:], x_send.at[0])
    take(back.at[:, 1:], b_send.at[0])


def last_kernel(acc, grads, wall, out_h, outs, sem):
    cols = slice((3 * PAIRS - 2) * PAIR, 3 * PAIRS * PAIR)
    copies = []
    for n in range(acc.shape[0]):
        rows = slice(n * CHUNK, (n + 1) * CHUNK)
        outs[n] = (acc[n] + dot(grads[:, cols], wall[rows, cols], 1, 1)).astype(BF16)
        copies.append(pltpu.make_async_copy(outs.at[n], out_h.at[:, rows], sem.at[n]))
        copies[n].start()
    for copy in copies:
        copy.wait()


def shards(tokens, cotangent, w_query, w_key, w_value, w_out):
    rows, width = tokens.shape
    blocks = lax.axis_size("ctxa") * lax.axis_size("ctxb")
    factor = 1.0 / math.sqrt(DH * rows * blocks)
    slot = (2, ROWS, DH)
    messages = 2 * PAIRS
    dma = pltpu.SemaphoreType.DMA
    steps = width // CHUNK
    parts = pl.pallas_call(
        functools.partial(kernel, factor),
        out_shape=[
            pltpu.VMEM((steps, rows, CHUNK), F32),
            pltpu.VMEM((rows, 3 * PAIRS * PAIR), BF16),
            pltpu.VMEM((width, 3 * PAIRS * PAIR), BF16),
        ],
        in_specs=[pl.BlockSpec(memory_space=pl.ANY)] * 6,
        out_specs=[pl.BlockSpec(memory_space=pltpu.VMEM)] * 3,
        scratch_shapes=[
            pltpu.VMEM((rows, width), BF16),
            pltpu.VMEM((rows, width), BF16),
            pltpu.VMEM((PAIRS * PAIR, width), BF16),
            pltpu.VMEM((PAIRS, 4, rows, PAIR), BF16),
            pltpu.VMEM((PAIRS, 3, rows, PAIR), F32),
            pltpu.VMEM((messages, 2, DH, DH), F32),
            pltpu.VMEM((messages, 2, NG, ROWS, DH), BF16),
            pltpu.VMEM((messages, NG, *slot), BF16),
            pltpu.VMEM((messages, NZ, 2, *slot), BF16),
            pltpu.VMEM((messages, *slot), BF16),
            pltpu.VMEM((messages, NX, *slot), BF16),
            pltpu.VMEM((messages, NG, *slot), BF16),
            pltpu.VMEM((messages, 2, NG, ROWS, DH), BF16),
            dma((4 * PAIRS + 2 * PARTS,)),
            *[dma((1,)), dma((messages,))] * 4,
        ],
        compiler_params=pltpu.CompilerParams(
            collective_id=0, has_side_effects=True, vmem_limit_bytes=40 * 1024 * 1024
        ),
    )(tokens, cotangent, w_query, w_key, w_value, w_out)
    return pl.pallas_call(
        last_kernel,
        out_shape=jax.ShapeDtypeStruct((rows, width), BF16),
        in_specs=[pl.BlockSpec(memory_space=pltpu.VMEM)] * 3,
        out_specs=pl.BlockSpec(memory_space=pl.ANY),
        scratch_shapes=[pltpu.VMEM((steps, rows, CHUNK), BF16), dma((steps,))],
        compiler_params=pltpu.CompilerParams(vmem_limit_bytes=16 * 1024 * 1024),
    )(*parts)


def solution(mesh):
    placed = (P(("ctxa", "ctxb"), None), P(("ctxa", "ctxb"), None), P(), P(), P(), P())
    return jax.shard_map(
        shards, mesh=mesh, in_specs=placed, out_specs=P(("ctxa", "ctxb"), None), check_vma=False
    )
```
